32 devices in a mesh: tr: 4 (over y, x), tc: 8 (over z, core).
Axes of the slice: x: 2, y: 2, z: 4, core: 2. Of those that a mesh axis runs over, the one named last changes fastest.
Arguments:
- green_function: float32 [2, 256, 256, 256], P(None, None, 'tr', 'tc'), may hold values from -6 to 6
Outputs:
- collision: float32 [2, 256, 256, 256], P(None, ('tr', 'tc'))
The draws below stay inside these ranges and needn't reach their ends.
All inputs are finite; a program needn't handle non-finite values.
Results may differ from the reference program's by a relative error of at most 0.00016.
Values sent between devices are 32-bit elements; how exact they have to be, the bound alone decides.
No kernel may reach another device: no remote copies, remote signals or barrier semaphores. Data moves between devices by JAX's collectives and lax.ppermute only.
A program may use at most 128 MiB of HBM per device.

```python
import math
import jax
import jax.numpy as jnp
from jax import lax

MOMENTA = 256
WINDOW = 256


def level_of(stream_key, shape, cuts, smallest, largest):
    def one(position, shards_of):
        draws = jax.random.uniform(jax.random.fold_in(jax.random.fold_in(stream_key, 6), position), (shards_of,), jnp.float32, smallest / len(cuts), largest / len(cuts))
        return jnp.repeat(jnp.exp(draws), shape[position] // shards_of).reshape((-1,) + (1,) * (len(shape) - position - 1))

    gain = one(*cuts[0])
    for cut in cuts[1:]:
        gain = gain * one(*cut)
    return gain


def normal_values(own_key, extent, spread, most, split=(), kind=jnp.bfloat16):
    loudness = level_of(own_key, extent, split, -0.22, 0.18) if split else 1.0
    values = jax.random.normal(own_key, extent, jnp.float32) * spread * loudness
    return jnp.minimum(jnp.maximum(values, -most), most).astype(kind)


def setup_inputs(seed: int = 0) -> dict:
    arg_keys = jax.random.split(jax.random.key(seed), 2)
    return {
        "green_function": normal_values(arg_keys[0], (2, MOMENTA, WINDOW, WINDOW), 1.0, 6.0, ((2, 4), (3, 8)), jnp.float32),
    }


coupling = 4.0
time_step = 0.2


def phase_tables(momenta, sites):
    wave_index = jnp.arange(momenta, dtype=jnp.int32)
    phase_index = (sites[:, None] * wave_index[None, :]) % momenta
    angles = phase_index.astype(jnp.float32) * (2.0 * math.pi / momenta)
    return jnp.cos(angles), jnp.sin(angles)


def reference(green_function):
    block_rows = 32
    site_index = jnp.arange(MOMENTA, dtype=jnp.int32)
    cos_table, sin_table = phase_tables(MOMENTA, site_index)
    neg_index = ((MOMENTA - site_index) % MOMENTA).astype(jnp.int32)
    highest = lax.Precision.HIGHEST

    def to_sites(values):
        real_part = (jnp.dot(cos_table, values[0], precision=highest) - jnp.dot(sin_table, values[1], precision=highest)) / MOMENTA
        imag_part = (jnp.dot(sin_table, values[0], precision=highest) + jnp.dot(cos_table, values[1], precision=highest)) / MOMENTA
        return jnp.stack([real_part, imag_part])

    def to_momenta(values):
        real_part = jnp.dot(cos_table.T, values[0], precision=highest) + jnp.dot(sin_table.T, values[1], precision=highest)
        imag_part = jnp.dot(cos_table.T, values[1], precision=highest) - jnp.dot(sin_table.T, values[0], precision=highest)
        return jnp.stack([real_part, imag_part])

    def row_block(start):
        row_part = lax.dynamic_slice_in_dim(green_function, start, block_rows, 2)
        col_part = lax.dynamic_slice_in_dim(green_function, start, block_rows, 3)
        site_rows = to_sites(row_part.reshape(2, MOMENTA, block_rows * WINDOW)).reshape(2, MOMENTA, block_rows, WINDOW)
        site_cols = to_sites(col_part.reshape(2, MOMENTA, WINDOW * block_rows)).reshape(2, MOMENTA, WINDOW, block_rows)
        mirror = jnp.swapaxes(site_cols[:, neg_index], 2, 3)
        square_re = site_rows[0] * site_rows[0] - site_rows[1] * site_rows[1]
        square_im = 2.0 * site_rows[0] * site_rows[1]
        strength = coupling * coupling
        sigma_re = strength * (square_re * mirror[0] - square_im * mirror[1])
        sigma_im = strength * (square_re * mirror[1] + square_im * mirror[0])
        site_sigma = jnp.stack([sigma_re, sigma_im]).reshape(2, MOMENTA, block_rows * WINDOW)
        sigma = to_momenta(site_sigma).reshape(2, MOMENTA, block_rows, WINDOW)
        real_part = jnp.einsum("kts,ksu->ktu", sigma[0], green_function[0], precision=highest) - jnp.einsum("kts,ksu->ktu", sigma[1], green_function[1], precision=highest)
        imag_part = jnp.einsum("kts,ksu->ktu", sigma[0], green_function[1], precision=highest) + jnp.einsum("kts,ksu->ktu", sigma[1], green_function[0], precision=highest)
        return time_step * jnp.stack([real_part, imag_part])

    starts = jnp.arange(0, WINDOW, block_rows, dtype=jnp.int32)
    blocks = lax.map(row_block, starts)
    return jnp.transpose(blocks, (1, 2, 0, 3, 4)).reshape(2, MOMENTA, WINDOW, WINDOW)
```

```python
import functools
import math

import jax
import jax.numpy as jnp
import numpy as np
from jax import lax
from jax.experimental import pallas as pl
from jax.experimental.pallas import tpu as pltpu
from jax.sharding import PartitionSpec as P

coupling = 4.0
time_step = 0.2
f32 = jnp.float32
bf16 = jnp.bfloat16
LANES = 128
SUBLANES = 8


def site_order(momenta, per_device):
    positions = jnp.arange(momenta, dtype=jnp.int32)
    half_slots = per_device // 2
    owner_index = positions // per_device
    slot_in_device = positions % per_device
    base_site = owner_index * half_slots + slot_in_device % half_slots
    mirrored = jnp.where(base_site == 0, momenta // 2, momenta - base_site)
    return jnp.where(slot_in_device < half_slots, base_site, mirrored)


def phase_tables(momenta, sites):
    wave_index = jnp.arange(momenta, dtype=jnp.int32)
    phase_index = sites[:, None] * wave_index[None, :] % momenta
    angles = phase_index.astype(jnp.float32) * (2.0 * math.pi / momenta)
    return (jnp.cos(angles), jnp.sin(angles))


def forward_matrix(cosine_table, sine_table, momenta):
    return (
        jnp.concatenate(
            [
                jnp.concatenate([cosine_table, -sine_table], 1),
                jnp.concatenate([sine_table, cosine_table], 1),
            ],
            0,
        )
        / momenta
    )


def inverse_matrix(cosine_table, sine_table):
    return jnp.concatenate(
        [
            jnp.concatenate([cosine_table.T, sine_table.T], 1),
            jnp.concatenate([-sine_table.T, cosine_table.T], 1),
        ],
        0,
    )


def cubic_product(site_full, mirror):
    square_re = site_full[0] * site_full[0] - site_full[1] * site_full[1]
    square_im = 2.0 * site_full[0] * site_full[1]
    strength = coupling * coupling
    sigma_re = strength * (square_re * mirror[0] - square_im * mirror[1])
    sigma_im = strength * (square_re * mirror[1] + square_im * mirror[0])
    return jnp.stack([sigma_re, sigma_im])


def general_shards(green_function):
    highest = lax.Precision.HIGHEST
    rows_count = lax.axis_size("tr")
    cols_count = lax.axis_size("tc")
    devices = rows_count * cols_count
    momenta = green_function.shape[1]
    tile_rows = green_function.shape[2]
    tile_cols = green_function.shape[3]
    window = tile_rows * rows_count
    per_device = momenta // devices
    half_slots = per_device // 2
    cells = tile_rows * tile_cols
    ratio = cols_count // rows_count
    green_split = green_function.reshape(2, devices, per_device, cells)
    cosine_table, sine_table = phase_tables(momenta, site_order(momenta, per_device))
    forward = forward_matrix(cosine_table, sine_table, momenta)
    site_tiles = jnp.dot(
        forward, green_function.reshape(2 * momenta, cells), precision=highest
    ).reshape(2, devices, per_device, cells)
    arrived = lax.all_to_all(site_tiles, ("tr", "tc"), split_axis=1, concat_axis=1, tiled=True)
    item_count = arrived.shape[2]
    shaped = arrived.reshape(2, rows_count, cols_count, item_count, tile_rows, tile_cols)
    site_full = shaped.transpose(0, 3, 1, 4, 2, 5).reshape(2, item_count, window, window)
    device = lax.axis_index("tr") * cols_count + lax.axis_index("tc")
    slot_index = jnp.arange(per_device, dtype=jnp.int32)
    self_mirror = (device == 0) & ((slot_index == 0) | (slot_index == half_slots))
    swapped = jnp.concatenate([site_full[:, half_slots:], site_full[:, :half_slots]], 1)
    mirror = jnp.swapaxes(jnp.where(self_mirror[None, :, None, None], site_full, swapped), 2, 3)
    site_sigma = cubic_product(site_full, mirror)
    outgoing = (
        site_sigma.reshape(2, per_device, rows_count, tile_rows, cols_count, tile_cols)
        .transpose(0, 2, 4, 1, 3, 5)
        .reshape(2, devices, per_device, cells)
    )
    returned = lax.all_to_all(outgoing, ("tr", "tc"), split_axis=1, concat_axis=1, tiled=True)
    inverse = inverse_matrix(cosine_table, sine_table)
    sigma_tiles = jnp.dot(inverse, returned.reshape(2 * momenta, cells), precision=highest).reshape(
        2, devices, per_device, cells
    )
    sigma_pieces = lax.all_to_all(
        sigma_tiles, ("tr", "tc"), split_axis=1, concat_axis=1, tiled=True
    )
    item_count = sigma_pieces.shape[2]
    sigma = sigma_pieces.reshape(2, rows_count, rows_count, ratio, item_count, tile_rows, tile_cols)
    green = lax.all_to_all(
        green_split, ("tr", "tc"), split_axis=1, concat_axis=1, tiled=True
    ).reshape(2, rows_count, cols_count, item_count, ratio, tile_cols, tile_cols)
    form = "agjktx,gDkjxu->katDu"
    real_part = jnp.einsum(form, sigma[0], green[0], precision=highest) - jnp.einsum(
        form, sigma[1], green[1], precision=highest
    )
    imag_part = jnp.einsum(form, sigma[0], green[1], precision=highest) + jnp.einsum(
        form, sigma[1], green[0], precision=highest
    )
    stacked = jnp.stack([real_part, imag_part])
    return time_step * stacked.reshape(2, item_count, window, window)


def kept_half(a, b):
    z, c = b // 2, b % 2
    return 1 - c if a < z else c if a > z else 0


def partner(a, b):
    z, c = b // 2, b % 2
    return (z, 2 * a + c) if a < z else (z, 2 * a + 1 - c)


def block_plan(rows_count):
    cols_count = 2 * rows_count
    route = []
    held = {}
    for a in range(rows_count):
        for b in range(cols_count):
            source = a * cols_count + b
            pa, pb = partner(a, b)
            target = pa * cols_count + pb
            keep = kept_half(a, b)
            route.append((source, target))
            held[(2 * a + keep, b)] = (source, 0)
            held[(2 * a + 1 - keep, b)] = (target, 1)
    return route, held


def split(x):
    high = x.astype(bf16)
    return high, (x - high.astype(f32)).astype(bf16)


def dot(x, y, dims=((1,), (0,))):
    return lax.dot_general(x, y, (dims, ((), ())), preferred_element_type=f32)


def dot3(x, y, dims=((1,), (0,))):
    return dot(x[0], y[0], dims) + dot(x[0], y[1], dims) + dot(x[1], y[0], dims)


def regroup(x):
    lane = lax.broadcasted_iota(jnp.int32, x[0].shape, 1)
    upper = lane >= LANES // 2
    odd = (lane // (LANES // 4)) % 2 == 1
    half, quarter = LANES // 2, LANES // 4

    def swap(p, q, mask, shift):
        return (
            jnp.where(mask, pltpu.roll(q, shift, 1), p),
            jnp.where(mask, q, pltpu.roll(p, LANES - shift, 1)),
        )

    a0, a2 = swap(x[0], x[2], upper, half)
    a1, a3 = swap(x[1], x[3], upper, half)
    y0, y1 = swap(a0, a1, odd, quarter)
    y2, y3 = swap(a2, a3, odd, quarter)
    return y0, y1, y2, y3


def send_kernel(x_ref, out_ref):
    spans = out_ref.shape[2]
    for v in range(spans):
        rows = jnp.concatenate([x_ref[0, spans * q + v] for q in range(4)], 0)
        out_ref[:, 0, v] = rows.T.reshape(out_ref.shape[0], SUBLANES, LANES)


def pack_green(x):
    comps, rows, cols, momenta = x.shape
    spans = rows * cols // LANES
    devices = momenta // SUBLANES
    parts = momenta // LANES
    return pl.pallas_call(
        send_kernel,
        grid=(comps, parts),
        in_specs=[pl.BlockSpec((1, rows, cols, LANES), lambda c, p: (c, 0, 0, p))],
        out_specs=pl.BlockSpec(
            (devices // parts, 1, spans, SUBLANES, LANES), lambda c, p: (p, c, 0, 0, 0)
        ),
        out_shape=jax.ShapeDtypeStruct((devices, comps, spans, SUBLANES, LANES), f32),
        cost_estimate=pl.CostEstimate(flops=0, bytes_accessed=2 * x.size * 4, transcendentals=0),
        name="pack_green",
    )(x)


def sigma_kernel(flags, kept_ref, other_ref, fh_ref, fl_ref, ih_ref, il_ref, out_ref, plus, minus):
    points, momenta = kept_ref.shape[2], kept_ref.shape[3]
    edge = math.isqrt(points)
    spans = points // LANES
    chunk = 256
    forward = (fh_ref[...], fl_ref[...])

    for unit, ref in ((0, kept_ref.at[:, 0]), (1, other_ref)):

        def transform(n, carry, unit=unit, ref=ref):
            rows = pl.ds(pl.multiple_of(n * chunk, chunk), chunk)
            y_re = dot3(split(ref[0, rows, :]), forward)
            y_im = dot3(split(ref[1, rows, :]), forward)
            re_c, re_s = y_re[:, :momenta], y_re[:, momenta:]
            im_c, im_s = y_im[:, :momenta], y_im[:, momenta:]
            plus[unit, 0, rows, :] = re_c - im_s
            plus[unit, 1, rows, :] = re_s + im_c
            m_re = re_c + im_s
            m_im = im_c - re_s
            for p in range(momenta // LANES):
                lanes = slice(LANES * p, LANES * (p + 1))
                minus[unit, 0, p, rows, :] = m_re[:, lanes]
                minus[unit, 1, p, rows, :] = m_im[:, lanes]
            return carry

        lax.fori_loop(0, points // chunk, transform, 0)

    inverse = (ih_ref[...], il_ref[...])
    diagonal = flags[1]
    for unit in range(2):
        facing = jnp.where(diagonal == 1, unit, 1 - unit)

        def combine(n, carry, unit=unit, facing=facing):
            s_re, s_im = [], []
            for w in range(2):
                for q in range(4):
                    i = spans * q + 2 * n + w
                    rows = pl.ds(pl.multiple_of(i * edge, edge), edge)
                    across = pl.ds(i, edge, stride=edge)
                    p_re, p_im = plus[unit, 0, rows, :], plus[unit, 1, rows, :]
                    m_re, m_im = (
                        jnp.concatenate(
                            [minus[facing, c, p, across, :] for p in range(momenta // LANES)], 1
                        )
                        for c in range(2)
                    )
                    sq_re = p_re * p_re - p_im * p_im
                    sq_im = 2.0 * p_re * p_im
                    s_re.append(sq_re * m_re - sq_im * m_im)
                    s_im.append(sq_re * m_im + sq_im * m_re)
            nt = ((1,), (1,))
            t_re = dot3(inverse, split(jnp.concatenate(s_re, 0)), nt)
            t_im = dot3(inverse, split(jnp.concatenate(s_im, 0)), nt)
            o_re = t_re[:momenta] + t_im[momenta:]
            o_im = t_im[:momenta] - t_re[momenta:]
            for w in range(2):
                lanes = slice(LANES * w, LANES * (w + 1))
                place = spans * unit + 2 * n + w
                shape = (momenta // SUBLANES, SUBLANES, LANES)
                out_ref[:, 0, place] = o_re[:, lanes].reshape(shape)
                out_ref[:, 1, place] = o_im[:, lanes].reshape(shape)
            return carry

        lax.fori_loop(0, spans // 2, combine, 0)


def form_sigma(flags, x, other, tables):
    comps, halves, points, momenta = x.shape
    devices = momenta // SUBLANES
    spans = 2 * points // LANES
    whole = lambda a: pl.BlockSpec(a.shape, lambda n, s: (0,) * a.ndim)
    flops = 3 * 2 * 4 * 2 * (2 * points) * momenta * momenta
    return pl.pallas_call(
        sigma_kernel,
        grid_spec=pltpu.PrefetchScalarGridSpec(
            num_scalar_prefetch=1,
            grid=(1,),
            in_specs=[
                pl.BlockSpec((comps, 1, points, momenta), lambda n, s: (0, s[0], 0, 0)),
                whole(other),
                *[whole(t) for t in tables],
            ],
            out_specs=pl.BlockSpec(
                (devices, comps, spans, SUBLANES, LANES), lambda n, s: (0, 0, 0, 0, 0)
            ),
            scratch_shapes=[
                pltpu.VMEM((2, comps, points, momenta), f32),
                pltpu.VMEM((2, comps, momenta // LANES, points, LANES), f32),
            ],
        ),
        out_shape=jax.ShapeDtypeStruct((devices, comps, spans, SUBLANES, LANES), f32),
        cost_estimate=pl.CostEstimate(
            flops=flops, bytes_accessed=3 * other.size * 4, transcendentals=0
        ),
        compiler_params=pltpu.CompilerParams(vmem_limit_bytes=56 * 1024 * 1024),
        name="form_sigma",
    )(flags, x, other, *tables)


def green_kernel(x_ref, out_ref, *, rows_count):
    cols_count = 2 * rows_count
    k = pl.program_id(0)
    tile_rows = out_ref.shape[3] // rows_count
    step = tile_rows // 4
    for comp in range(2):
        for a in range(rows_count):
            for side in range(cols_count // 4):
                groups = [[] for _ in range(4)]
                for part in range(step // SUBLANES):
                    span = pl.ds(SUBLANES * SUBLANES * part + k, SUBLANES, stride=SUBLANES)
                    loaded = [
                        x_ref[a * cols_count + 4 * side + n, comp, span, :] for n in range(4)
                    ]
                    for q, value in enumerate(regroup(loaded)):
                        groups[q].append(value)
                for q in range(4):
                    high, low = split(jnp.concatenate(groups[q], 0))
                    rows = slice(tile_rows * a + step * q, tile_rows * a + step * (q + 1))
                    lanes = slice(LANES * side, LANES * (side + 1))
                    out_ref[0, comp, 0, rows, lanes] = high
                    out_ref[0, comp, 1, rows, lanes] = low


def arrange_green(x, rows_count, window):
    x = x.reshape(x.shape[0], 2, -1, LANES)
    return pl.pallas_call(
        functools.partial(green_kernel, rows_count=rows_count),
        grid=(SUBLANES,),
        in_specs=[pl.BlockSpec(x.shape, lambda k: (0, 0, 0, 0))],
        out_specs=pl.BlockSpec((1, 2, 2, window, window), lambda k: (k, 0, 0, 0, 0)),
        out_shape=jax.ShapeDtypeStruct((SUBLANES, 2, 2, window, window), bf16),
        cost_estimate=pl.CostEstimate(flops=0, bytes_accessed=2 * x.size * 4, transcendentals=0),
        name="arrange_green",
    )(x)


def collide_kernel(s_ref, g_ref, out_ref, left, *, held, blocks):
    k = pl.program_id(0)
    edge = out_ref.shape[2] // blocks
    for comp in range(2):
        for row in range(blocks):
            for side in range(blocks // 4):
                loaded = []
                for n in range(4):
                    source, unit = held[(row, 4 * side + n)]
                    span = pl.ds(SUBLANES * SUBLANES * unit + k, SUBLANES, stride=SUBLANES)
                    loaded.append(s_ref[source, comp, span, :])
                high, low = split(jnp.concatenate(regroup(loaded), 0))
                rows = slice(edge * row, edge * (row + 1))
                lanes = slice(LANES * side, LANES * (side + 1))
                left[comp, 0, rows, lanes] = high
                left[comp, 1, rows, lanes] = low
    re, im = ((left[c, 0], left[c, 1]) for c in range(2))
    g_re, g_im = ((g_ref[0, c, 0], g_ref[0, c, 1]) for c in range(2))
    out_ref[0, 0] = time_step * (dot3(re, g_re) - dot3(im, g_im))
    out_ref[1, 0] = time_step * (dot3(re, g_im) + dot3(im, g_re))


def collide(sigma, green, held, blocks):
    window = green.shape[-1]
    sigma = sigma.reshape(sigma.shape[0], 2, -1, LANES)
    return pl.pallas_call(
        functools.partial(collide_kernel, held=held, blocks=blocks),
        grid=(SUBLANES,),
        in_specs=[
            pl.BlockSpec(sigma.shape, lambda k: (0, 0, 0, 0)),
            pl.BlockSpec((1, 2, 2, window, window), lambda k: (k, 0, 0, 0, 0)),
        ],
        out_specs=pl.BlockSpec((2, 1, window, window), lambda k: (0, k, 0, 0)),
        out_shape=jax.ShapeDtypeStruct((2, SUBLANES, window, window), f32),
        scratch_shapes=[pltpu.VMEM((2, 2, window, window), bf16)],
        cost_estimate=pl.CostEstimate(
            flops=3 * 8 * SUBLANES * window**3, bytes_accessed=3 * sigma.size * 4, transcendentals=0
        ),
        name="collide",
    )(sigma, green)


def table_pair(values):
    high = values.astype(np.float32).astype(bf16)
    low = (values - high.astype(np.float64)).astype(np.float32).astype(bf16)
    return jnp.asarray(high), jnp.asarray(low)


def dft_tables(momenta):
    index = np.arange(momenta)
    angle = 2.0 * np.pi * (index[:, None] * index[None, :] % momenta) / momenta
    cosine, sine = np.cos(angle), np.sin(angle)
    strength = coupling * coupling / momenta**3
    forward = np.concatenate([cosine, sine], 1)
    inverse = strength * np.concatenate([cosine, sine], 0)
    return (*table_pair(forward), *table_pair(inverse))


def packed_shards(green_function):
    axes = ("tr", "tc")
    rows_count = lax.axis_size("tr")
    comps, momenta, tile_rows, tile_cols = green_function.shape
    window = tile_rows * rows_count
    points = tile_cols * tile_cols
    route, held = block_plan(rows_count)
    a = lax.axis_index("tr")
    b = lax.axis_index("tc")
    z, c = b // 2, b % 2
    keep = jnp.where(a < z, 1 - c, jnp.where(a > z, c, 0)).astype(jnp.int32)
    diagonal = ((a == z) & (c == 0)).astype(jnp.int32)

    x = green_function.transpose(0, 2, 3, 1)
    halves = x.reshape(comps, 2, points, momenta)
    leaving = lax.dynamic_index_in_dim(halves, 1 - keep, 1, keepdims=False)
    other = lax.ppermute(leaving, axes, route)
    green = lax.all_to_all(pack_green(x), axes, split_axis=0, concat_axis=0, tiled=True)
    tables = dft_tables(momenta)
    sigma = form_sigma(jnp.stack([keep, diagonal]), halves, other, tables)
    sigma = lax.all_to_all(sigma, axes, split_axis=0, concat_axis=0, tiled=True)
    green = arrange_green(green, rows_count, window)
    return collide(sigma, green, held, 2 * rows_count)


def shards(green_function):
    rows_count = lax.axis_size("tr")
    cols_count = lax.axis_size("tc")
    comps, momenta, tile_rows, tile_cols = green_function.shape
    packs = (
        cols_count == 2 * rows_count
        and tile_rows == 2 * tile_cols
        and 4 * tile_cols == LANES
        and momenta == SUBLANES * rows_count * cols_count
        and momenta % LANES == 0
        and cols_count % 4 == 0
    )
    return packed_shards(green_function) if packs else general_shards(green_function)


def solution(mesh):
    return jax.shard_map(
        shards,
        mesh=mesh,
        in_specs=(P(None, None, "tr", "tc"),),
        out_specs=P(None, ("tr", "tc"), None, None),
        check_vma=False,
    )
```

```python
import functools
import math

import jax
import jax.numpy as jnp
import numpy as np
from jax import lax
from jax.experimental import pallas as pl
from jax.experimental.pallas import tpu as pltpu
from jax.sharding import PartitionSpec as P

coupling = 4.0
time_step = 0.2
f32 = jnp.float32
bf16 = jnp.bfloat16
LANES = 128
SUBLANES = 8


def site_order(momenta, per_device):
    positions = jnp.arange(momenta, dtype=jnp.int32)
    half_slots = per_device // 2
    owner_index = positions // per_device
    slot_in_device = positions % per_device
    base_site = owner_index * half_slots + slot_in_device % half_slots
    mirrored = jnp.where(base_site == 0, momenta // 2, momenta - base_site)
    return jnp.where(slot_in_device < half_slots, base_site, mirrored)


def phase_tables(momenta, sites):
    wave_index = jnp.arange(momenta, dtype=jnp.int32)
    phase_index = sites[:, None] * wave_index[None, :] % momenta
    angles = phase_index.astype(jnp.float32) * (2.0 * math.pi / momenta)
    return (jnp.cos(angles), jnp.sin(angles))


def forward_matrix(cosine_table, sine_table, momenta):
    return (
        jnp.concatenate(
            [
                jnp.concatenate([cosine_table, -sine_table], 1),
                jnp.concatenate([sine_table, cosine_table], 1),
            ],
            0,
        )
        / momenta
    )


def inverse_matrix(cosine_table, sine_table):
    return jnp.concatenate(
        [
            jnp.concatenate([cosine_table.T, sine_table.T], 1),
            jnp.concatenate([-sine_table.T, cosine_table.T], 1),
        ],
        0,
    )


def cubic_product(site_full, mirror):
    square_re = site_full[0] * site_full[0] - site_full[1] * site_full[1]
    square_im = 2.0 * site_full[0] * site_full[1]
    strength = coupling * coupling
    sigma_re = strength * (square_re * mirror[0] - square_im * mirror[1])
    sigma_im = strength * (square_re * mirror[1] + square_im * mirror[0])
    return jnp.stack([sigma_re, sigma_im])


def general_shards(green_function):
    highest = lax.Precision.HIGHEST
    rows_count = lax.axis_size("tr")
    cols_count = lax.axis_size("tc")
    devices = rows_count * cols_count
    momenta = green_function.shape[1]
    tile_rows = green_function.shape[2]
    tile_cols = green_function.shape[3]
    window = tile_rows * rows_count
    per_device = momenta // devices
    half_slots = per_device // 2
    cells = tile_rows * tile_cols
    ratio = cols_count // rows_count
    green_split = green_function.reshape(2, devices, per_device, cells)
    cosine_table, sine_table = phase_tables(momenta, site_order(momenta, per_device))
    forward = forward_matrix(cosine_table, sine_table, momenta)
    site_tiles = jnp.dot(
        forward, green_function.reshape(2 * momenta, cells), precision=highest
    ).reshape(2, devices, per_device, cells)
    arrived = lax.all_to_all(site_tiles, ("tr", "tc"), split_axis=1, concat_axis=1, tiled=True)
    item_count = arrived.shape[2]
    shaped = arrived.reshape(2, rows_count, cols_count, item_count, tile_rows, tile_cols)
    site_full = shaped.transpose(0, 3, 1, 4, 2, 5).reshape(2, item_count, window, window)
    device = lax.axis_index("tr") * cols_count + lax.axis_index("tc")
    slot_index = jnp.arange(per_device, dtype=jnp.int32)
    self_mirror = (device == 0) & ((slot_index == 0) | (slot_index == half_slots))
    swapped = jnp.concatenate([site_full[:, half_slots:], site_full[:, :half_slots]], 1)
    mirror = jnp.swapaxes(jnp.where(self_mirror[None, :, None, None], site_full, swapped), 2, 3)
    site_sigma = cubic_product(site_full, mirror)
    outgoing = (
        site_sigma.reshape(2, per_device, rows_count, tile_rows, cols_count, tile_cols)
        .transpose(0, 2, 4, 1, 3, 5)
        .reshape(2, devices, per_device, cells)
    )
    returned = lax.all_to_all(outgoing, ("tr", "tc"), split_axis=1, concat_axis=1, tiled=True)
    inverse = inverse_matrix(cosine_table, sine_table)
    sigma_tiles = jnp.dot(inverse, returned.reshape(2 * momenta, cells), precision=highest).reshape(
        2, devices, per_device, cells
    )
    sigma_pieces = lax.all_to_all(
        sigma_tiles, ("tr", "tc"), split_axis=1, concat_axis=1, tiled=True
    )
    item_count = sigma_pieces.shape[2]
    sigma = sigma_pieces.reshape(2, rows_count, rows_count, ratio, item_count, tile_rows, tile_cols)
    green = lax.all_to_all(
        green_split, ("tr", "tc"), split_axis=1, concat_axis=1, tiled=True
    ).reshape(2, rows_count, cols_count, item_count, ratio, tile_cols, tile_cols)
    form = "agjktx,gDkjxu->katDu"
    real_part = jnp.einsum(form, sigma[0], green[0], precision=highest) - jnp.einsum(
        form, sigma[1], green[1], precision=highest
    )
    imag_part = jnp.einsum(form, sigma[0], green[1], precision=highest) + jnp.einsum(
        form, sigma[1], green[0], precision=highest
    )
    stacked = jnp.stack([real_part, imag_part])
    return time_step * stacked.reshape(2, item_count, window, window)


def kept_half(a, b):
    z, c = b // 2, b % 2
    return 1 - c if a < z else c if a > z else 0


def partner(a, b):
    z, c = b // 2, b % 2
    return (z, 2 * a + c) if a < z else (z, 2 * a + 1 - c)


def relay(a, b, rows_count):
    return (a + rows_count // 2) % rows_count, b


def block_plan(rows_count):
    cols_count = 2 * rows_count
    route, first, second = [], [], []
    held = {}
    for a in range(rows_count):
        for b in range(cols_count):
            source = a * cols_count + b
            pa, pb = partner(a, b)
            target = pa * cols_count + pb
            keep = kept_half(a, b)
            ra, rb = relay(a, b, rows_count)
            middle = ra * cols_count + rb
            route.append((source, target))
            first.append((source, middle))
            second.append((middle, target))
            held[(2 * a + keep, b)] = (source, 0)
            held[(2 * a + 1 - keep, b)] = (target, 1)
    return route, first, second, held


def split(x):
    high = x.astype(bf16)
    return high, (x - high.astype(f32)).astype(bf16)


def dot(x, y, dims=((1,), (0,))):
    return lax.dot_general(x, y, (dims, ((), ())), preferred_element_type=f32)


def dot3(x, y, dims=((1,), (0,))):
    return dot(x[0], y[0], dims) + dot(x[0], y[1], dims) + dot(x[1], y[0], dims)


def regroup(x):
    lane = lax.broadcasted_iota(jnp.int32, x[0].shape, 1)
    upper = lane >= LANES // 2
    odd = (lane // (LANES // 4)) % 2 == 1
    half, quarter = LANES // 2, LANES // 4

    def swap(p, q, mask, shift):
        return (
            jnp.where(mask, pltpu.roll(q, shift, 1), p),
            jnp.where(mask, q, pltpu.roll(p, LANES - shift, 1)),
        )

    a0, a2 = swap(x[0], x[2], upper, half)
    a1, a3 = swap(x[1], x[3], upper, half)
    y0, y1 = swap(a0, a1, odd, quarter)
    y2, y3 = swap(a2, a3, odd, quarter)
    return y0, y1, y2, y3


def send_kernel(x_ref, out_ref):
    spans = out_ref.shape[2]
    for v in range(spans):
        rows = jnp.concatenate([x_ref[0, spans * q + v] for q in range(4)], 0)
        out_ref[:, 0, v] = rows.T.reshape(out_ref.shape[0], SUBLANES, LANES)


def pack_green(x):
    comps, rows, cols, momenta = x.shape
    spans = rows * cols // LANES
    devices = momenta // SUBLANES
    parts = momenta // LANES
    return pl.pallas_call(
        send_kernel,
        grid=(comps, parts),
        in_specs=[pl.BlockSpec((1, rows, cols, LANES), lambda c, p: (c, 0, 0, p))],
        out_specs=pl.BlockSpec(
            (devices // parts, 1, spans, SUBLANES, LANES), lambda c, p: (p, c, 0, 0, 0)
        ),
        out_shape=jax.ShapeDtypeStruct((devices, comps, spans, SUBLANES, LANES), f32),
        cost_estimate=pl.CostEstimate(flops=0, bytes_accessed=2 * x.size * 4, transcendentals=0),
        name="pack_green",
    )(x)


def sigma_kernel(flags, kept_ref, re_ref, im_ref, fh_ref, fl_ref, ih_ref, il_ref, out_ref, plus, minus):
    points, momenta = kept_ref.shape[2], kept_ref.shape[3]
    edge = math.isqrt(points)
    spans = points // LANES
    chunk = 256
    forward = (fh_ref[...], fl_ref[...])

    for unit, refs in enumerate(((kept_ref.at[0, 0], kept_ref.at[1, 0]), (re_ref, im_ref))):

        def transform(n, carry, unit=unit, refs=refs):
            rows = pl.ds(pl.multiple_of(n * chunk, chunk), chunk)
            y_re = dot3(split(refs[0][rows, :]), forward)
            y_im = dot3(split(refs[1][rows, :]), forward)
            re_c, re_s = y_re[:, :momenta], y_re[:, momenta:]
            im_c, im_s = y_im[:, :momenta], y_im[:, momenta:]
            plus[unit, 0, rows, :] = re_c - im_s
            plus[unit, 1, rows, :] = re_s + im_c
            m_re = re_c + im_s
            m_im = im_c - re_s
            for p in range(momenta // LANES):
                lanes = slice(LANES * p, LANES * (p + 1))
                minus[unit, 0, p, rows, :] = m_re[:, lanes]
                minus[unit, 1, p, rows, :] = m_im[:, lanes]
            return carry

        lax.fori_loop(0, points // chunk, transform, 0)

    inverse = (ih_ref[...], il_ref[...])
    diagonal = flags[1]
    for unit in range(2):
        facing = jnp.where(diagonal == 1, unit, 1 - unit)

        def combine(n, carry, unit=unit, facing=facing):
            s_re, s_im = [], []
            for w in range(2):
                for q in range(4):
                    i = spans * q + 2 * n + w
                    rows = pl.ds(pl.multiple_of(i * edge, edge), edge)
                    across = pl.ds(i, edge, stride=edge)
                    p_re, p_im = plus[unit, 0, rows, :], plus[unit, 1, rows, :]
                    m_re, m_im = (
                        jnp.concatenate(
                            [minus[facing, c, p, across, :] for p in range(momenta // LANES)], 1
                        )
                        for c in range(2)
                    )
                    sq_re = p_re * p_re - p_im * p_im
                    sq_im = 2.0 * p_re * p_im
                    s_re.append(sq_re * m_re - sq_im * m_im)
                    s_im.append(sq_re * m_im + sq_im * m_re)
            nt = ((1,), (1,))
            t_re = dot3(inverse, split(jnp.concatenate(s_re, 0)), nt)
            t_im = dot3(inverse, split(jnp.concatenate(s_im, 0)), nt)
            o_re = t_re[:momenta] + t_im[momenta:]
            o_im = t_im[:momenta] - t_re[momenta:]
            for w in range(2):
                lanes = slice(LANES * w, LANES * (w + 1))
                place = spans * unit + 2 * n + w
                shape = (momenta // SUBLANES, SUBLANES, LANES)
                out_ref[:, 0, place] = o_re[:, lanes].reshape(shape)
                out_ref[:, 1, place] = o_im[:, lanes].reshape(shape)
            return carry

        lax.fori_loop(0, spans // 2, combine, 0)


def form_sigma(flags, x, other_re, other_im, tables):
    comps, _, points, momenta = x.shape
    devices = momenta // SUBLANES
    spans = 2 * points // LANES
    whole = lambda a: pl.BlockSpec(a.shape, lambda n, s: (0,) * a.ndim)
    flops = 3 * 2 * 4 * 2 * (2 * points) * momenta * momenta
    return pl.pallas_call(
        sigma_kernel,
        grid_spec=pltpu.PrefetchScalarGridSpec(
            num_scalar_prefetch=1,
            grid=(1,),
            in_specs=[
                pl.BlockSpec((comps, 1, points, momenta), lambda n, s: (0, s[0], 0, 0)),
                whole(other_re),
                whole(other_im),
                *[whole(t) for t in tables],
            ],
            out_specs=pl.BlockSpec(
                (devices, comps, spans, SUBLANES, LANES), lambda n, s: (0, 0, 0, 0, 0)
            ),
            scratch_shapes=[
                pltpu.VMEM((2, comps, points, momenta), f32),
                pltpu.VMEM((2, comps, momenta // LANES, points, LANES), f32),
            ],
        ),
        out_shape=jax.ShapeDtypeStruct((devices, comps, spans, SUBLANES, LANES), f32),
        cost_estimate=pl.CostEstimate(
            flops=flops, bytes_accessed=6 * other_re.size * 4, transcendentals=0
        ),
        compiler_params=pltpu.CompilerParams(vmem_limit_bytes=56 * 1024 * 1024),
        name="form_sigma",
    )(flags, x, other_re, other_im, *tables)


def green_kernel(x_ref, out_ref, *, rows_count):
    cols_count = 2 * rows_count
    k = pl.program_id(0)
    tile_rows = out_ref.shape[3] // rows_count
    step = tile_rows // 4
    for comp in range(2):
        for a in range(rows_count):
            for side in range(cols_count // 4):
                groups = [[] for _ in range(4)]
                for part in range(step // SUBLANES):
                    span = pl.ds(SUBLANES * SUBLANES * part + k, SUBLANES, stride=SUBLANES)
                    loaded = [
                        x_ref[a * cols_count + 4 * side + n, comp, span, :] for n in range(4)
                    ]
                    for q, value in enumerate(regroup(loaded)):
                        groups[q].append(value)
                for q in range(4):
                    high, low = split(jnp.concatenate(groups[q], 0))
                    rows = slice(tile_rows * a + step * q, tile_rows * a + step * (q + 1))
                    lanes = slice(LANES * side, LANES * (side + 1))
                    out_ref[0, comp, 0, rows, lanes] = high
                    out_ref[0, comp, 1, rows, lanes] = low


def arrange_green(x, rows_count, window):
    x = x.reshape(x.shape[0], 2, -1, LANES)
    return pl.pallas_call(
        functools.partial(green_kernel, rows_count=rows_count),
        grid=(SUBLANES,),
        in_specs=[pl.BlockSpec(x.shape, lambda k: (0, 0, 0, 0))],
        out_specs=pl.BlockSpec((1, 2, 2, window, window), lambda k: (k, 0, 0, 0, 0)),
        out_shape=jax.ShapeDtypeStruct((SUBLANES, 2, 2, window, window), bf16),
        cost_estimate=pl.CostEstimate(flops=0, bytes_accessed=2 * x.size * 4, transcendentals=0),
        name="arrange_green",
    )(x)


def collide_kernel(s_ref, g_ref, out_ref, left, *, held, blocks):
    k = pl.program_id(0)
    edge = out_ref.shape[2] // blocks
    for comp in range(2):
        for row in range(blocks):
            for side in range(blocks // 4):
                loaded = []
                for n in range(4):
                    source, unit = held[(row, 4 * side + n)]
                    span = pl.ds(SUBLANES * SUBLANES * unit + k, SUBLANES, stride=SUBLANES)
                    loaded.append(s_ref[source, comp, span, :])
                high, low = split(jnp.concatenate(regroup(loaded), 0))
                rows = slice(edge * row, edge * (row + 1))
                lanes = slice(LANES * side, LANES * (side + 1))
                left[comp, 0, rows, lanes] = high
                left[comp, 1, rows, lanes] = low
    re, im = ((left[c, 0], left[c, 1]) for c in range(2))
    g_re, g_im = ((g_ref[0, c, 0], g_ref[0, c, 1]) for c in range(2))
    out_ref[0, 0] = time_step * (dot3(re, g_re) - dot3(im, g_im))
    out_ref[1, 0] = time_step * (dot3(re, g_im) + dot3(im, g_re))


def collide(sigma, green, held, blocks):
    window = green.shape[-1]
    sigma = sigma.reshape(sigma.shape[0], 2, -1, LANES)
    return pl.pallas_call(
        functools.partial(collide_kernel, held=held, blocks=blocks),
        grid=(SUBLANES,),
        in_specs=[
            pl.BlockSpec(sigma.shape, lambda k: (0, 0, 0, 0)),
            pl.BlockSpec((1, 2, 2, window, window), lambda k: (k, 0, 0, 0, 0)),
        ],
        out_specs=pl.BlockSpec((2, 1, window, window), lambda k: (0, k, 0, 0)),
        out_shape=jax.ShapeDtypeStruct((2, SUBLANES, window, window), f32),
        scratch_shapes=[pltpu.VMEM((2, 2, window, window), bf16)],
        cost_estimate=pl.CostEstimate(
            flops=3 * 8 * SUBLANES * window**3, bytes_accessed=3 * sigma.size * 4, transcendentals=0
        ),
        name="collide",
    )(sigma, green)


def table_pair(values):
    high = values.astype(np.float32).astype(bf16)
    low = (values - high.astype(np.float64)).astype(np.float32).astype(bf16)
    return jnp.asarray(high), jnp.asarray(low)


def dft_tables(momenta):
    index = np.arange(momenta)
    angle = 2.0 * np.pi * (index[:, None] * index[None, :] % momenta) / momenta
    cosine, sine = np.cos(angle), np.sin(angle)
    strength = coupling * coupling / momenta**3
    forward = np.concatenate([cosine, sine], 1)
    inverse = strength * np.concatenate([cosine, sine], 0)
    return (*table_pair(forward), *table_pair(inverse))


def packed_shards(green_function):
    axes = ("tr", "tc")
    rows_count = lax.axis_size("tr")
    comps, momenta, tile_rows, tile_cols = green_function.shape
    window = tile_rows * rows_count
    points = tile_cols * tile_cols
    route, first, second, held = block_plan(rows_count)
    a = lax.axis_index("tr")
    b = lax.axis_index("tc")
    z, c = b // 2, b % 2
    keep = jnp.where(a < z, 1 - c, jnp.where(a > z, c, 0)).astype(jnp.int32)
    diagonal = ((a == z) & (c == 0)).astype(jnp.int32)

    x = green_function.transpose(0, 2, 3, 1)
    halves = x.reshape(comps, 2, points, momenta)
    leaving = [
        lax.dynamic_slice(halves, (n, 1 - keep, 0, 0), (1, 1, points, momenta)).reshape(
            points, momenta
        )
        for n in range(comps)
    ]
    tables = dft_tables(momenta)
    other_im = lax.ppermute(leaving[1], axes, first)
    other_re = lax.ppermute(leaving[0], axes, route)
    other_im = lax.ppermute(other_im, axes, second)
    packed = pack_green(x)
    green = lax.all_to_all(packed, axes, split_axis=0, concat_axis=0, tiled=True)
    sigma = form_sigma(jnp.stack([keep, diagonal]), halves, other_re, other_im, tables)
    sigma = lax.all_to_all(sigma, axes, split_axis=0, concat_axis=0, tiled=True)
    green = arrange_green(green, rows_count, window)
    return collide(sigma, green, held, 2 * rows_count)


def is_packed(rows_count, cols_count, comps, momenta, tile_rows, tile_cols):
    return (
        cols_count == 2 * rows_count
        and tile_rows == 2 * tile_cols
        and 4 * tile_cols == LANES
        and momenta == SUBLANES * rows_count * cols_count
        and momenta % LANES == 0
        and cols_count % 4 == 0
    )


def shards(green_function):
    sizes = (lax.axis_size("tr"), lax.axis_size("tc"), *green_function.shape)
    return packed_shards(green_function) if is_packed(*sizes) else general_shards(green_function)


def solution(mesh):
    return jax.shard_map(
        shards,
        mesh=mesh,
        in_specs=(P(None, None, "tr", "tc"),),
        out_specs=P(None, ("tr", "tc"), None, None),
        check_vma=False,
    )
```

```python
import functools
import math

import jax
import jax.numpy as jnp
import numpy as np
from jax import lax
from jax.experimental import pallas as pl
from jax.experimental.pallas import tpu as pltpu
from jax.sharding import PartitionSpec as P

coupling = 4.0
time_step = 0.2
f32 = jnp.float32
bf16 = jnp.bfloat16
LANES = 128
SUBLANES = 8


def site_order(momenta, per_device):
    positions = jnp.arange(momenta, dtype=jnp.int32)
    half_slots = per_device // 2
    owner_index = positions // per_device
    slot_in_device = positions % per_device
    base_site = owner_index * half_slots + slot_in_device % half_slots
    mirrored = jnp.where(base_site == 0, momenta // 2, momenta - base_site)
    return jnp.where(slot_in_device < half_slots, base_site, mirrored)


def phase_tables(momenta, sites):
    wave_index = jnp.arange(momenta, dtype=jnp.int32)
    phase_index = sites[:, None] * wave_index[None, :] % momenta
    angles = phase_index.astype(jnp.float32) * (2.0 * math.pi / momenta)
    return (jnp.cos(angles), jnp.sin(angles))


def forward_matrix(cosine_table, sine_table, momenta):
    return (
        jnp.concatenate(
            [
                jnp.concatenate([cosine_table, -sine_table], 1),
                jnp.concatenate([sine_table, cosine_table], 1),
            ],
            0,
        )
        / momenta
    )


def inverse_matrix(cosine_table, sine_table):
    return jnp.concatenate(
        [
            jnp.concatenate([cosine_table.T, sine_table.T], 1),
            jnp.concatenate([-sine_table.T, cosine_table.T], 1),
        ],
        0,
    )


def cubic_product(site_full, mirror):
    square_re = site_full[0] * site_full[0] - site_full[1] * site_full[1]
    square_im = 2.0 * site_full[0] * site_full[1]
    strength = coupling * coupling
    sigma_re = strength * (square_re * mirror[0] - square_im * mirror[1])
    sigma_im = strength * (square_re * mirror[1] + square_im * mirror[0])
    return jnp.stack([sigma_re, sigma_im])


def general_shards(green_function):
    highest = lax.Precision.HIGHEST
    rows_count = lax.axis_size("tr")
    cols_count = lax.axis_size("tc")
    devices = rows_count * cols_count
    momenta = green_function.shape[1]
    tile_rows = green_function.shape[2]
    tile_cols = green_function.shape[3]
    window = tile_rows * rows_count
    per_device = momenta // devices
    half_slots = per_device // 2
    cells = tile_rows * tile_cols
    ratio = cols_count // rows_count
    green_split = green_function.reshape(2, devices, per_device, cells)
    cosine_table, sine_table = phase_tables(momenta, site_order(momenta, per_device))
    forward = forward_matrix(cosine_table, sine_table, momenta)
    site_tiles = jnp.dot(
        forward, green_function.reshape(2 * momenta, cells), precision=highest
    ).reshape(2, devices, per_device, cells)
    arrived = lax.all_to_all(site_tiles, ("tr", "tc"), split_axis=1, concat_axis=1, tiled=True)
    item_count = arrived.shape[2]
    shaped = arrived.reshape(2, rows_count, cols_count, item_count, tile_rows, tile_cols)
    site_full = shaped.transpose(0, 3, 1, 4, 2, 5).reshape(2, item_count, window, window)
    device = lax.axis_index("tr") * cols_count + lax.axis_index("tc")
    slot_index = jnp.arange(per_device, dtype=jnp.int32)
    self_mirror = (device == 0) & ((slot_index == 0) | (slot_index == half_slots))
    swapped = jnp.concatenate([site_full[:, half_slots:], site_full[:, :half_slots]], 1)
    mirror = jnp.swapaxes(jnp.where(self_mirror[None, :, None, None], site_full, swapped), 2, 3)
    site_sigma = cubic_product(site_full, mirror)
    outgoing = (
        site_sigma.reshape(2, per_device, rows_count, tile_rows, cols_count, tile_cols)
        .transpose(0, 2, 4, 1, 3, 5)
        .reshape(2, devices, per_device, cells)
    )
    returned = lax.all_to_all(outgoing, ("tr", "tc"), split_axis=1, concat_axis=1, tiled=True)
    inverse = inverse_matrix(cosine_table, sine_table)
    sigma_tiles = jnp.dot(inverse, returned.reshape(2 * momenta, cells), precision=highest).reshape(
        2, devices, per_device, cells
    )
    sigma_pieces = lax.all_to_all(
        sigma_tiles, ("tr", "tc"), split_axis=1, concat_axis=1, tiled=True
    )
    item_count = sigma_pieces.shape[2]
    sigma = sigma_pieces.reshape(2, rows_count, rows_count, ratio, item_count, tile_rows, tile_cols)
    green = lax.all_to_all(
        green_split, ("tr", "tc"), split_axis=1, concat_axis=1, tiled=True
    ).reshape(2, rows_count, cols_count, item_count, ratio, tile_cols, tile_cols)
    form = "agjktx,gDkjxu->katDu"
    real_part = jnp.einsum(form, sigma[0], green[0], precision=highest) - jnp.einsum(
        form, sigma[1], green[1], precision=highest
    )
    imag_part = jnp.einsum(form, sigma[0], green[1], precision=highest) + jnp.einsum(
        form, sigma[1], green[0], precision=highest
    )
    stacked = jnp.stack([real_part, imag_part])
    return time_step * stacked.reshape(2, item_count, window, window)


def kept_half(a, b):
    z, c = b // 2, b % 2
    return 1 - c if a < z else c if a > z else 0


def partner(a, b):
    z, c = b // 2, b % 2
    return (z, 2 * a + c) if a < z else (z, 2 * a + 1 - c)


def relay(a, b, rows_count):
    return (a + rows_count // 2) % rows_count, b


def block_plan(rows_count):
    cols_count = 2 * rows_count
    route, first, second = [], [], []
    held = {}
    for a in range(rows_count):
        for b in range(cols_count):
            source = a * cols_count + b
            pa, pb = partner(a, b)
            target = pa * cols_count + pb
            keep = kept_half(a, b)
            ra, rb = relay(a, b, rows_count)
            middle = ra * cols_count + rb
            route.append((source, target))
            first.append((source, middle))
            second.append((middle, target))
            held[(2 * a + keep, b)] = (source, 0)
            held[(2 * a + 1 - keep, b)] = (target, 1)
    return route, first, second, held


def split(x):
    high = x.astype(bf16)
    return high, (x - high.astype(f32)).astype(bf16)


def dot(x, y, dims=((1,), (0,))):
    return lax.dot_general(x, y, (dims, ((), ())), preferred_element_type=f32)


def dot3(x, y, dims=((1,), (0,))):
    return dot(x[0], y[0], dims) + dot(x[0], y[1], dims) + dot(x[1], y[0], dims)


def regroup(x):
    lane = lax.broadcasted_iota(jnp.int32, x[0].shape, 1)
    upper = lane >= LANES // 2
    odd = (lane // (LANES // 4)) % 2 == 1
    half, quarter = LANES // 2, LANES // 4

    def swap(p, q, mask, shift):
        return (
            jnp.where(mask, pltpu.roll(q, shift, 1), p),
            jnp.where(mask, q, pltpu.roll(p, LANES - shift, 1)),
        )

    a0, a2 = swap(x[0], x[2], upper, half)
    a1, a3 = swap(x[1], x[3], upper, half)
    y0, y1 = swap(a0, a1, odd, quarter)
    y2, y3 = swap(a2, a3, odd, quarter)
    return y0, y1, y2, y3


def send_kernel(x_ref, out_ref):
    spans = out_ref.shape[1]
    for v in range(spans):
        rows = jnp.concatenate([x_ref[0, spans * q + v] for q in range(4)], 0)
        out_ref[:, v] = rows.T.reshape(out_ref.shape[0], SUBLANES, LANES)


def pack_green(x, comp):
    _, rows, cols, momenta = x.shape
    spans = rows * cols // LANES
    devices = momenta // SUBLANES
    parts = momenta // LANES
    return pl.pallas_call(
        send_kernel,
        grid=(parts,),
        in_specs=[pl.BlockSpec((1, rows, cols, LANES), lambda p: (comp, 0, 0, p))],
        out_specs=pl.BlockSpec((devices // parts, spans, SUBLANES, LANES), lambda p: (p, 0, 0, 0)),
        out_shape=jax.ShapeDtypeStruct((devices, spans, SUBLANES, LANES), f32),
        cost_estimate=pl.CostEstimate(flops=0, bytes_accessed=x.size * 4, transcendentals=0),
        name="pack_green",
    )(x)


def sigma_kernel(flags, kept_ref, re_ref, im_ref, fh_ref, fl_ref, ih_ref, il_ref, out_ref, plus, minus):
    points, momenta = kept_ref.shape[2], kept_ref.shape[3]
    edge = math.isqrt(points)
    spans = points // LANES
    chunk = 256
    forward = (fh_ref[...], fl_ref[...])

    for unit, refs in enumerate(((kept_ref.at[0, 0], kept_ref.at[1, 0]), (re_ref, im_ref))):

        def transform(n, carry, unit=unit, refs=refs):
            rows = pl.ds(pl.multiple_of(n * chunk, chunk), chunk)
            y_re = dot3(split(refs[0][rows, :]), forward)
            y_im = dot3(split(refs[1][rows, :]), forward)
            re_c, re_s = y_re[:, :momenta], y_re[:, momenta:]
            im_c, im_s = y_im[:, :momenta], y_im[:, momenta:]
            plus[unit, 0, rows, :] = re_c - im_s
            plus[unit, 1, rows, :] = re_s + im_c
            m_re = re_c + im_s
            m_im = im_c - re_s
            for p in range(momenta // LANES):
                lanes = slice(LANES * p, LANES * (p + 1))
                minus[unit, 0, p, rows, :] = m_re[:, lanes]
                minus[unit, 1, p, rows, :] = m_im[:, lanes]
            return carry

        lax.fori_loop(0, points // chunk, transform, 0)

    inverse = (ih_ref[...], il_ref[...])
    diagonal = flags[1]
    for unit in range(2):
        facing = jnp.where(diagonal == 1, unit, 1 - unit)

        def combine(n, carry, unit=unit, facing=facing):
            s_re, s_im = [], []
            for w in range(2):
                for q in range(4):
                    i = spans * q + 2 * n + w
                    rows = pl.ds(pl.multiple_of(i * edge, edge), edge)
                    across = pl.ds(i, edge, stride=edge)
                    p_re, p_im = plus[unit, 0, rows, :], plus[unit, 1, rows, :]
                    m_re, m_im = (
                        jnp.concatenate(
                            [minus[facing, c, p, across, :] for p in range(momenta // LANES)], 1
                        )
                        for c in range(2)
                    )
                    sq_re = p_re * p_re - p_im * p_im
                    sq_im = 2.0 * p_re * p_im
                    s_re.append(sq_re * m_re - sq_im * m_im)
                    s_im.append(sq_re * m_im + sq_im * m_re)
            nt = ((1,), (1,))
            t_re = dot3(inverse, split(jnp.concatenate(s_re, 0)), nt)
            t_im = dot3(inverse, split(jnp.concatenate(s_im, 0)), nt)
            o_re = t_re[:momenta] + t_im[momenta:]
            o_im = t_im[:momenta] - t_re[momenta:]
            for w in range(2):
                lanes = slice(LANES * w, LANES * (w + 1))
                place = spans * unit + 2 * n + w
                shape = (momenta // SUBLANES, SUBLANES, LANES)
                out_ref[:, 0, place] = o_re[:, lanes].reshape(shape)
                out_ref[:, 1, place] = o_im[:, lanes].reshape(shape)
            return carry

        lax.fori_loop(0, spans // 2, combine, 0)


def form_sigma(flags, x, other_re, other_im, tables):
    comps, _, points, momenta = x.shape
    devices = momenta // SUBLANES
    spans = 2 * points // LANES
    whole = lambda a: pl.BlockSpec(a.shape, lambda n, s: (0,) * a.ndim)
    flops = 3 * 2 * 4 * 2 * (2 * points) * momenta * momenta
    return pl.pallas_call(
        sigma_kernel,
        grid_spec=pltpu.PrefetchScalarGridSpec(
            num_scalar_prefetch=1,
            grid=(1,),
            in_specs=[
                pl.BlockSpec((comps, 1, points, momenta), lambda n, s: (0, s[0], 0, 0)),
                whole(other_re),
                whole(other_im),
                *[whole(t) for t in tables],
            ],
            out_specs=pl.BlockSpec(
                (devices, comps, spans, SUBLANES, LANES), lambda n, s: (0, 0, 0, 0, 0)
            ),
            scratch_shapes=[
                pltpu.VMEM((2, comps, points, momenta), f32),
                pltpu.VMEM((2, comps, momenta // LANES, points, LANES), f32),
            ],
        ),
        out_shape=jax.ShapeDtypeStruct((devices, comps, spans, SUBLANES, LANES), f32),
        cost_estimate=pl.CostEstimate(
            flops=flops, bytes_accessed=6 * other_re.size * 4, transcendentals=0
        ),
        compiler_params=pltpu.CompilerParams(vmem_limit_bytes=56 * 1024 * 1024),
        name="form_sigma",
    )(flags, x, other_re, other_im, *tables)


def green_kernel(re_ref, im_ref, out_ref, *, rows_count):
    cols_count = 2 * rows_count
    k = pl.program_id(0)
    tile_rows = out_ref.shape[3] // rows_count
    step = tile_rows // 4
    for comp, x_ref in enumerate((re_ref, im_ref)):
        for a in range(rows_count):
            for side in range(cols_count // 4):
                groups = [[] for _ in range(4)]
                for part in range(step // SUBLANES):
                    span = pl.ds(SUBLANES * SUBLANES * part + k, SUBLANES, stride=SUBLANES)
                    loaded = [
                        x_ref[a * cols_count + 4 * side + n, span, :] for n in range(4)
                    ]
                    for q, value in enumerate(regroup(loaded)):
                        groups[q].append(value)
                for q in range(4):
                    high, low = split(jnp.concatenate(groups[q], 0))
                    rows = slice(tile_rows * a + step * q, tile_rows * a + step * (q + 1))
                    lanes = slice(LANES * side, LANES * (side + 1))
                    out_ref[0, comp, 0, rows, lanes] = high
                    out_ref[0, comp, 1, rows, lanes] = low


def arrange_green(parts, rows_count, window):
    parts = [x.reshape(x.shape[0], -1, LANES) for x in parts]
    return pl.pallas_call(
        functools.partial(green_kernel, rows_count=rows_count),
        grid=(SUBLANES,),
        in_specs=[pl.BlockSpec(x.shape, lambda k: (0, 0, 0)) for x in parts],
        out_specs=pl.BlockSpec((1, 2, 2, window, window), lambda k: (k, 0, 0, 0, 0)),
        out_shape=jax.ShapeDtypeStruct((SUBLANES, 2, 2, window, window), bf16),
        cost_estimate=pl.CostEstimate(
            flops=0, bytes_accessed=4 * parts[0].size * 4, transcendentals=0
        ),
        name="arrange_green",
    )(*parts)


def collide_kernel(s_ref, g_ref, out_ref, left, *, held, blocks):
    k = pl.program_id(0)
    edge = out_ref.shape[2] // blocks
    for comp in range(2):
        for row in range(blocks):
            for side in range(blocks // 4):
                loaded = []
                for n in range(4):
                    source, unit = held[(row, 4 * side + n)]
                    span = pl.ds(SUBLANES * SUBLANES * unit + k, SUBLANES, stride=SUBLANES)
                    loaded.append(s_ref[source, comp, span, :])
                high, low = split(jnp.concatenate(regroup(loaded), 0))
                rows = slice(edge * row, edge * (row + 1))
                lanes = slice(LANES * side, LANES * (side + 1))
                left[comp, 0, rows, lanes] = high
                left[comp, 1, rows, lanes] = low
    re, im = ((left[c, 0], left[c, 1]) for c in range(2))
    g_re, g_im = ((g_ref[0, c, 0], g_ref[0, c, 1]) for c in range(2))
    out_ref[0, 0] = time_step * (dot3(re, g_re) - dot3(im, g_im))
    out_ref[1, 0] = time_step * (dot3(re, g_im) + dot3(im, g_re))


def collide(sigma, green, held, blocks):
    window = green.shape[-1]
    sigma = sigma.reshape(sigma.shape[0], 2, -1, LANES)
    return pl.pallas_call(
        functools.partial(collide_kernel, held=held, blocks=blocks),
        grid=(SUBLANES,),
        in_specs=[
            pl.BlockSpec(sigma.shape, lambda k: (0, 0, 0, 0)),
            pl.BlockSpec((1, 2, 2, window, window), lambda k: (k, 0, 0, 0, 0)),
        ],
        out_specs=pl.BlockSpec((2, 1, window, window), lambda k: (0, k, 0, 0)),
        out_shape=jax.ShapeDtypeStruct((2, SUBLANES, window, window), f32),
        scratch_shapes=[pltpu.VMEM((2, 2, window, window), bf16)],
        cost_estimate=pl.CostEstimate(
            flops=3 * 8 * SUBLANES * window**3, bytes_accessed=3 * sigma.size * 4, transcendentals=0
        ),
        name="collide",
    )(sigma, green)


def table_pair(values):
    high = values.astype(np.float32).astype(bf16)
    low = (values - high.astype(np.float64)).astype(np.float32).astype(bf16)
    return jnp.asarray(high), jnp.asarray(low)


def dft_tables(momenta):
    index = np.arange(momenta)
    angle = 2.0 * np.pi * (index[:, None] * index[None, :] % momenta) / momenta
    cosine, sine = np.cos(angle), np.sin(angle)
    strength = coupling * coupling / momenta**3
    forward = np.concatenate([cosine, sine], 1)
    inverse = strength * np.concatenate([cosine, sine], 0)
    return (*table_pair(forward), *table_pair(inverse))


def packed_shards(green_function):
    axes = ("tr", "tc")
    rows_count = lax.axis_size("tr")
    comps, momenta, tile_rows, tile_cols = green_function.shape
    window = tile_rows * rows_count
    points = tile_cols * tile_cols
    route, first, second, held = block_plan(rows_count)
    a = lax.axis_index("tr")
    b = lax.axis_index("tc")
    z, c = b // 2, b % 2
    keep = jnp.where(a < z, 1 - c, jnp.where(a > z, c, 0)).astype(jnp.int32)
    diagonal = ((a == z) & (c == 0)).astype(jnp.int32)

    x = green_function.transpose(0, 2, 3, 1)
    halves = x.reshape(comps, 2, points, momenta)
    leaving = [
        lax.dynamic_slice(halves, (n, 1 - keep, 0, 0), (1, 1, points, momenta)).reshape(
            points, momenta
        )
        for n in range(comps)
    ]
    tables = dft_tables(momenta)
    other_im = lax.ppermute(leaving[1], axes, first)
    other_re = lax.ppermute(leaving[0], axes, route)
    other_im = lax.ppermute(other_im, axes, second)
    green = [pack_green(x, comp) for comp in range(comps)]
    for comp in range(comps):
        green[comp] = lax.all_to_all(green[comp], axes, split_axis=0, concat_axis=0, tiled=True)
    sigma = form_sigma(jnp.stack([keep, diagonal]), halves, other_re, other_im, tables)
    sigma = lax.all_to_all(sigma, axes, split_axis=0, concat_axis=0, tiled=True)
    green = arrange_green(green, rows_count, window)
    return collide(sigma, green, held, 2 * rows_count)


def is_packed(rows_count, cols_count, comps, momenta, tile_rows, tile_cols):
    return (
        cols_count == 2 * rows_count
        and tile_rows == 2 * tile_cols
        and 4 * tile_cols == LANES
        and momenta == SUBLANES * rows_count * cols_count
        and momenta % LANES == 0
        and cols_count % 4 == 0
    )


def shards(green_function):
    sizes = (lax.axis_size("tr"), lax.axis_size("tc"), *green_function.shape)
    return packed_shards(green_function) if is_packed(*sizes) else general_shards(green_function)


def solution(mesh):
    return jax.shard_map(
        shards,
        mesh=mesh,
        in_specs=(P(None, None, "tr", "tc"),),
        out_specs=P(None, ("tr", "tc"), None, None),
        check_vma=False,
    )
```

```python
import functools
import math

import jax
import jax.numpy as jnp
import numpy as np
from jax import lax
from jax.experimental import pallas as pl
from jax.experimental.pallas import tpu as pltpu
from jax.sharding import PartitionSpec as P

coupling = 4.0
time_step = 0.2
f32 = jnp.float32
bf16 = jnp.bfloat16
LANES = 128
SUBLANES = 8


def site_order(momenta, per_device):
    positions = jnp.arange(momenta, dtype=jnp.int32)
    half_slots = per_device // 2
    owner_index = positions // per_device
    slot_in_device = positions % per_device
    base_site = owner_index * half_slots + slot_in_device % half_slots
    mirrored = jnp.where(base_site == 0, momenta // 2, momenta - base_site)
    return jnp.where(slot_in_device < half_slots, base_site, mirrored)


def phase_tables(momenta, sites):
    wave_index = jnp.arange(momenta, dtype=jnp.int32)
    phase_index = sites[:, None] * wave_index[None, :] % momenta
    angles = phase_index.astype(jnp.float32) * (2.0 * math.pi / momenta)
    return (jnp.cos(angles), jnp.sin(angles))


def forward_matrix(cosine_table, sine_table, momenta):
    return (
        jnp.concatenate(
            [
                jnp.concatenate([cosine_table, -sine_table], 1),
                jnp.concatenate([sine_table, cosine_table], 1),
            ],
            0,
        )
        / momenta
    )


def inverse_matrix(cosine_table, sine_table):
    return jnp.concatenate(
        [
            jnp.concatenate([cosine_table.T, sine_table.T], 1),
            jnp.concatenate([-sine_table.T, cosine_table.T], 1),
        ],
        0,
    )


def cubic_product(site_full, mirror):
    square_re = site_full[0] * site_full[0] - site_full[1] * site_full[1]
    square_im = 2.0 * site_full[0] * site_full[1]
    strength = coupling * coupling
    sigma_re = strength * (square_re * mirror[0] - square_im * mirror[1])
    sigma_im = strength * (square_re * mirror[1] + square_im * mirror[0])
    return jnp.stack([sigma_re, sigma_im])


def general_shards(green_function):
    highest = lax.Precision.HIGHEST
    rows_count = lax.axis_size("tr")
    cols_count = lax.axis_size("tc")
    devices = rows_count * cols_count
    momenta = green_function.shape[1]
    tile_rows = green_function.shape[2]
    tile_cols = green_function.shape[3]
    window = tile_rows * rows_count
    per_device = momenta // devices
    half_slots = per_device // 2
    cells = tile_rows * tile_cols
    ratio = cols_count // rows_count
    green_split = green_function.reshape(2, devices, per_device, cells)
    cosine_table, sine_table = phase_tables(momenta, site_order(momenta, per_device))
    forward = forward_matrix(cosine_table, sine_table, momenta)
    site_tiles = jnp.dot(
        forward, green_function.reshape(2 * momenta, cells), precision=highest
    ).reshape(2, devices, per_device, cells)
    arrived = lax.all_to_all(site_tiles, ("tr", "tc"), split_axis=1, concat_axis=1, tiled=True)
    item_count = arrived.shape[2]
    shaped = arrived.reshape(2, rows_count, cols_count, item_count, tile_rows, tile_cols)
    site_full = shaped.transpose(0, 3, 1, 4, 2, 5).reshape(2, item_count, window, window)
    device = lax.axis_index("tr") * cols_count + lax.axis_index("tc")
    slot_index = jnp.arange(per_device, dtype=jnp.int32)
    self_mirror = (device == 0) & ((slot_index == 0) | (slot_index == half_slots))
    swapped = jnp.concatenate([site_full[:, half_slots:], site_full[:, :half_slots]], 1)
    mirror = jnp.swapaxes(jnp.where(self_mirror[None, :, None, None], site_full, swapped), 2, 3)
    site_sigma = cubic_product(site_full, mirror)
    outgoing = (
        site_sigma.reshape(2, per_device, rows_count, tile_rows, cols_count, tile_cols)
        .transpose(0, 2, 4, 1, 3, 5)
        .reshape(2, devices, per_device, cells)
    )
    returned = lax.all_to_all(outgoing, ("tr", "tc"), split_axis=1, concat_axis=1, tiled=True)
    inverse = inverse_matrix(cosine_table, sine_table)
    sigma_tiles = jnp.dot(inverse, returned.reshape(2 * momenta, cells), precision=highest).reshape(
        2, devices, per_device, cells
    )
    sigma_pieces = lax.all_to_all(
        sigma_tiles, ("tr", "tc"), split_axis=1, concat_axis=1, tiled=True
    )
    item_count = sigma_pieces.shape[2]
    sigma = sigma_pieces.reshape(2, rows_count, rows_count, ratio, item_count, tile_rows, tile_cols)
    green = lax.all_to_all(
        green_split, ("tr", "tc"), split_axis=1, concat_axis=1, tiled=True
    ).reshape(2, rows_count, cols_count, item_count, ratio, tile_cols, tile_cols)
    form = "agjktx,gDkjxu->katDu"
    real_part = jnp.einsum(form, sigma[0], green[0], precision=highest) - jnp.einsum(
        form, sigma[1], green[1], precision=highest
    )
    imag_part = jnp.einsum(form, sigma[0], green[1], precision=highest) + jnp.einsum(
        form, sigma[1], green[0], precision=highest
    )
    stacked = jnp.stack([real_part, imag_part])
    return time_step * stacked.reshape(2, item_count, window, window)


def kept_half(a, b):
    z, c = b // 2, b % 2
    return 1 - c if a < z else c if a > z else 0


def partner(a, b):
    z, c = b // 2, b % 2
    return (z, 2 * a + c) if a < z else (z, 2 * a + 1 - c)


def ways(rows_count):
    return (0, 1, rows_count // 2, rows_count // 2 + 1)


def block_plan(rows_count):
    cols_count = 2 * rows_count
    first = [[] for _ in ways(rows_count)]
    second = [[] for _ in ways(rows_count)]
    held = {}
    for a in range(rows_count):
        for b in range(cols_count):
            source = a * cols_count + b
            pa, pb = partner(a, b)
            target = pa * cols_count + pb
            for n, flip in enumerate(ways(rows_count)):
                middle = (a ^ flip) * cols_count + b
                first[n].append((source, middle))
                second[n].append((middle, target))
            keep = kept_half(a, b)
            held[(2 * a + keep, b)] = (source, 0)
            held[(2 * a + 1 - keep, b)] = (target, 1)
    return first, second, held


def split(x):
    high = x.astype(bf16)
    return high, (x - high.astype(f32)).astype(bf16)


def dot(x, y, dims=((1,), (0,))):
    return lax.dot_general(x, y, (dims, ((), ())), preferred_element_type=f32)


def dot3(x, y, dims=((1,), (0,))):
    return dot(x[0], y[0], dims) + dot(x[0], y[1], dims) + dot(x[1], y[0], dims)


def regroup(x):
    lane = lax.broadcasted_iota(jnp.int32, x[0].shape, 1)
    upper = lane >= LANES // 2
    odd = (lane // (LANES // 4)) % 2 == 1
    half, quarter = LANES // 2, LANES // 4

    def swap(p, q, mask, shift):
        return (
            jnp.where(mask, pltpu.roll(q, shift, 1), p),
            jnp.where(mask, q, pltpu.roll(p, LANES - shift, 1)),
        )

    a0, a2 = swap(x[0], x[2], upper, half)
    a1, a3 = swap(x[1], x[3], upper, half)
    y0, y1 = swap(a0, a1, odd, quarter)
    y2, y3 = swap(a2, a3, odd, quarter)
    return y0, y1, y2, y3


def send_kernel(x_ref, out_ref):
    spans = out_ref.shape[1]
    for v in range(spans):
        rows = jnp.concatenate([x_ref[0, spans * q + v] for q in range(4)], 0)
        out_ref[:, v] = rows.T.reshape(out_ref.shape[0], SUBLANES, LANES)


def pack_green(x, comp):
    _, rows, cols, momenta = x.shape
    spans = rows * cols // LANES
    devices = momenta // SUBLANES
    parts = momenta // LANES
    return pl.pallas_call(
        send_kernel,
        grid=(parts,),
        in_specs=[pl.BlockSpec((1, rows, cols, LANES), lambda p: (comp, 0, 0, p))],
        out_specs=pl.BlockSpec((devices // parts, spans, SUBLANES, LANES), lambda p: (p, 0, 0, 0)),
        out_shape=jax.ShapeDtypeStruct((devices, spans, SUBLANES, LANES), f32),
        cost_estimate=pl.CostEstimate(flops=0, bytes_accessed=x.size * 4, transcendentals=0),
        name="pack_green",
    )(x)


def sigma_kernel(flags, kept_ref, re0_ref, re1_ref, im0_ref, im1_ref, fh_ref, fl_ref, ih_ref, il_ref, out_ref, plus, minus):
    points, momenta = kept_ref.shape[2], kept_ref.shape[3]
    edge = math.isqrt(points)
    spans = points // LANES
    chunk = 256
    forward = (fh_ref[...], fl_ref[...])

    half = points // 2
    pieces = (
        (0, 0, points, kept_ref.at[0, 0], kept_ref.at[1, 0]),
        (1, 0, half, re0_ref, im0_ref),
        (1, half, half, re1_ref, im1_ref),
    )
    for unit, start, count, re_ref, im_ref in pieces:

        def transform(n, carry, unit=unit, start=start, re_ref=re_ref, im_ref=im_ref):
            source = pl.ds(pl.multiple_of(n * chunk, chunk), chunk)
            rows = pl.ds(pl.multiple_of(start + n * chunk, chunk), chunk)
            y_re = dot3(split(re_ref[source, :]), forward)
            y_im = dot3(split(im_ref[source, :]), forward)
            re_c, re_s = y_re[:, :momenta], y_re[:, momenta:]
            im_c, im_s = y_im[:, :momenta], y_im[:, momenta:]
            plus[unit, 0, rows, :] = re_c - im_s
            plus[unit, 1, rows, :] = re_s + im_c
            m_re = re_c + im_s
            m_im = im_c - re_s
            for p in range(momenta // LANES):
                lanes = slice(LANES * p, LANES * (p + 1))
                minus[unit, 0, p, rows, :] = m_re[:, lanes]
                minus[unit, 1, p, rows, :] = m_im[:, lanes]
            return carry

        lax.fori_loop(0, count // chunk, transform, 0)

    inverse = (ih_ref[...], il_ref[...])
    diagonal = flags[1]
    for unit in range(2):
        facing = jnp.where(diagonal == 1, unit, 1 - unit)

        def combine(n, carry, unit=unit, facing=facing):
            s_re, s_im = [], []
            for w in range(2):
                for q in range(4):
                    i = spans * q + 2 * n + w
                    rows = pl.ds(pl.multiple_of(i * edge, edge), edge)
                    across = pl.ds(i, edge, stride=edge)
                    p_re, p_im = plus[unit, 0, rows, :], plus[unit, 1, rows, :]
                    m_re, m_im = (
                        jnp.concatenate(
                            [minus[facing, c, p, across, :] for p in range(momenta // LANES)], 1
                        )
                        for c in range(2)
                    )
                    sq_re = p_re * p_re - p_im * p_im
                    sq_im = 2.0 * p_re * p_im
                    s_re.append(sq_re * m_re - sq_im * m_im)
                    s_im.append(sq_re * m_im + sq_im * m_re)
            nt = ((1,), (1,))
            t_re = dot3(inverse, split(jnp.concatenate(s_re, 0)), nt)
            t_im = dot3(inverse, split(jnp.concatenate(s_im, 0)), nt)
            o_re = t_re[:momenta] + t_im[momenta:]
            o_im = t_im[:momenta] - t_re[momenta:]
            for w in range(2):
                lanes = slice(LANES * w, LANES * (w + 1))
                place = spans * unit + 2 * n + w
                shape = (momenta // SUBLANES, SUBLANES, LANES)
                out_ref[:, 0, place] = o_re[:, lanes].reshape(shape)
                out_ref[:, 1, place] = o_im[:, lanes].reshape(shape)
            return carry

        lax.fori_loop(0, spans // 2, combine, 0)


def form_sigma(flags, x, others, tables):
    comps, _, points, momenta = x.shape
    devices = momenta // SUBLANES
    spans = 2 * points // LANES
    whole = lambda a: pl.BlockSpec(a.shape, lambda n, s: (0,) * a.ndim)
    flops = 3 * 2 * 4 * 2 * (2 * points) * momenta * momenta
    return pl.pallas_call(
        sigma_kernel,
        grid_spec=pltpu.PrefetchScalarGridSpec(
            num_scalar_prefetch=1,
            grid=(1,),
            in_specs=[
                pl.BlockSpec((comps, 1, points, momenta), lambda n, s: (0, s[0], 0, 0)),
                *[whole(t) for t in others],
                *[whole(t) for t in tables],
            ],
            out_specs=pl.BlockSpec(
                (devices, comps, spans, SUBLANES, LANES), lambda n, s: (0, 0, 0, 0, 0)
            ),
            scratch_shapes=[
                pltpu.VMEM((2, comps, points, momenta), f32),
                pltpu.VMEM((2, comps, momenta // LANES, points, LANES), f32),
            ],
        ),
        out_shape=jax.ShapeDtypeStruct((devices, comps, spans, SUBLANES, LANES), f32),
        cost_estimate=pl.CostEstimate(
            flops=flops, bytes_accessed=12 * others[0].size * 4, transcendentals=0
        ),
        compiler_params=pltpu.CompilerParams(vmem_limit_bytes=56 * 1024 * 1024),
        name="form_sigma",
    )(flags, x, *others, *tables)


def green_kernel(re_ref, im_ref, out_ref, *, rows_count):
    cols_count = 2 * rows_count
    k = pl.program_id(0)
    tile_rows = out_ref.shape[3] // rows_count
    step = tile_rows // 4
    for comp, x_ref in enumerate((re_ref, im_ref)):
        for a in range(rows_count):
            for side in range(cols_count // 4):
                groups = [[] for _ in range(4)]
                for part in range(step // SUBLANES):
                    span = pl.ds(SUBLANES * SUBLANES * part + k, SUBLANES, stride=SUBLANES)
                    loaded = [
                        x_ref[a * cols_count + 4 * side + n, span, :] for n in range(4)
                    ]
                    for q, value in enumerate(regroup(loaded)):
                        groups[q].append(value)
                for q in range(4):
                    high, low = split(jnp.concatenate(groups[q], 0))
                    rows = slice(tile_rows * a + step * q, tile_rows * a + step * (q + 1))
                    lanes = slice(LANES * side, LANES * (side + 1))
                    out_ref[0, comp, 0, rows, lanes] = high
                    out_ref[0, comp, 1, rows, lanes] = low


def arrange_green(parts, rows_count, window):
    parts = [x.reshape(x.shape[0], -1, LANES) for x in parts]
    return pl.pallas_call(
        functools.partial(green_kernel, rows_count=rows_count),
        grid=(SUBLANES,),
        in_specs=[pl.BlockSpec(x.shape, lambda k: (0, 0, 0)) for x in parts],
        out_specs=pl.BlockSpec((1, 2, 2, window, window), lambda k: (k, 0, 0, 0, 0)),
        out_shape=jax.ShapeDtypeStruct((SUBLANES, 2, 2, window, window), bf16),
        cost_estimate=pl.CostEstimate(
            flops=0, bytes_accessed=4 * parts[0].size * 4, transcendentals=0
        ),
        name="arrange_green",
    )(*parts)


def collide_kernel(s_ref, g_ref, out_ref, left, *, held, blocks):
    k = pl.program_id(0)
    edge = out_ref.shape[2] // blocks
    for comp in range(2):
        for row in range(blocks):
            for side in range(blocks // 4):
                loaded = []
                for n in range(4):
                    source, unit = held[(row, 4 * side + n)]
                    span = pl.ds(SUBLANES * SUBLANES * unit + k, SUBLANES, stride=SUBLANES)
                    loaded.append(s_ref[source, comp, span, :])
                high, low = split(jnp.concatenate(regroup(loaded), 0))
                rows = slice(edge * row, edge * (row + 1))
                lanes = slice(LANES * side, LANES * (side + 1))
                left[comp, 0, rows, lanes] = high
                left[comp, 1, rows, lanes] = low
    re, im = ((left[c, 0], left[c, 1]) for c in range(2))
    g_re, g_im = ((g_ref[0, c, 0], g_ref[0, c, 1]) for c in range(2))
    out_ref[0, 0] = time_step * (dot3(re, g_re) - dot3(im, g_im))
    out_ref[1, 0] = time_step * (dot3(re, g_im) + dot3(im, g_re))


def collide(sigma, green, held, blocks):
    window = green.shape[-1]
    sigma = sigma.reshape(sigma.shape[0], 2, -1, LANES)
    return pl.pallas_call(
        functools.partial(collide_kernel, held=held, blocks=blocks),
        grid=(SUBLANES,),
        in_specs=[
            pl.BlockSpec(sigma.shape, lambda k: (0, 0, 0, 0)),
            pl.BlockSpec((1, 2, 2, window, window), lambda k: (k, 0, 0, 0, 0)),
        ],
        out_specs=pl.BlockSpec((2, 1, window, window), lambda k: (0, k, 0, 0)),
        out_shape=jax.ShapeDtypeStruct((2, SUBLANES, window, window), f32),
        scratch_shapes=[pltpu.VMEM((2, 2, window, window), bf16)],
        cost_estimate=pl.CostEstimate(
            flops=3 * 8 * SUBLANES * window**3, bytes_accessed=3 * sigma.size * 4, transcendentals=0
        ),
        name="collide",
    )(sigma, green)


def table_pair(values):
    high = values.astype(np.float32).astype(bf16)
    low = (values - high.astype(np.float64)).astype(np.float32).astype(bf16)
    return jnp.asarray(high), jnp.asarray(low)


def dft_tables(momenta):
    index = np.arange(momenta)
    angle = 2.0 * np.pi * (index[:, None] * index[None, :] % momenta) / momenta
    cosine, sine = np.cos(angle), np.sin(angle)
    strength = coupling * coupling / momenta**3
    forward = np.concatenate([cosine, sine], 1)
    inverse = strength * np.concatenate([cosine, sine], 0)
    return (*table_pair(forward), *table_pair(inverse))


def packed_shards(green_function):
    axes = ("tr", "tc")
    rows_count = lax.axis_size("tr")
    comps, momenta, tile_rows, tile_cols = green_function.shape
    window = tile_rows * rows_count
    points = tile_cols * tile_cols
    first, second, held = block_plan(rows_count)
    a = lax.axis_index("tr")
    b = lax.axis_index("tc")
    z, c = b // 2, b % 2
    keep = jnp.where(a < z, 1 - c, jnp.where(a > z, c, 0)).astype(jnp.int32)
    diagonal = ((a == z) & (c == 0)).astype(jnp.int32)

    x = green_function.transpose(0, 2, 3, 1)
    halves = x.reshape(comps, 2, points, momenta)
    half = points // 2
    leaving = [
        lax.dynamic_slice(
            halves, (n // 2, 1 - keep, half * (n % 2), 0), (1, 1, half, momenta)
        ).reshape(half, momenta)
        for n in range(4)
    ]
    tables = dft_tables(momenta)
    others = list(leaving)
    for n in range(1, 4):
        others[n] = lax.ppermute(others[n], axes, first[n])
    for n in range(4):
        others[n] = lax.ppermute(others[n], axes, second[n])
    green = [pack_green(x, comp) for comp in range(comps)]
    for comp in range(comps):
        green[comp] = lax.all_to_all(green[comp], axes, split_axis=0, concat_axis=0, tiled=True)
    sigma = form_sigma(jnp.stack([keep, diagonal]), halves, others, tables)
    sigma = lax.all_to_all(sigma, axes, split_axis=0, concat_axis=0, tiled=True)
    green = arrange_green(green, rows_count, window)
    return collide(sigma, green, held, 2 * rows_count)


def is_packed(rows_count, cols_count, comps, momenta, tile_rows, tile_cols):
    return (
        cols_count == 2 * rows_count
        and tile_rows == 2 * tile_cols
        and 4 * tile_cols == LANES
        and momenta == SUBLANES * rows_count * cols_count
        and momenta % LANES == 0
        and cols_count % 4 == 0
        and rows_count & (rows_count - 1) == 0
    )


def shards(green_function):
    sizes = (lax.axis_size("tr"), lax.axis_size("tc"), *green_function.shape)
    return packed_shards(green_function) if is_packed(*sizes) else general_shards(green_function)


def solution(mesh):
    return jax.shard_map(
        shards,
        mesh=mesh,
        in_specs=(P(None, None, "tr", "tc"),),
        out_specs=P(None, ("tr", "tc"), None, None),
        check_vma=False,
    )
```

```python
import functools
import math

import jax
import jax.numpy as jnp
import numpy as np
from jax import lax
from jax.experimental import pallas as pl
from jax.experimental.pallas import tpu as pltpu
from jax.sharding import PartitionSpec as P

coupling = 4.0
time_step = 0.2
f32 = jnp.float32
bf16 = jnp.bfloat16
LANES = 128
SUBLANES = 8


def site_order(momenta, per_device):
    positions = jnp.arange(momenta, dtype=jnp.int32)
    half_slots = per_device // 2
    owner_index = positions // per_device
    slot_in_device = positions % per_device
    base_site = owner_index * half_slots + slot_in_device % half_slots
    mirrored = jnp.where(base_site == 0, momenta // 2, momenta - base_site)
    return jnp.where(slot_in_device < half_slots, base_site, mirrored)


def phase_tables(momenta, sites):
    wave_index = jnp.arange(momenta, dtype=jnp.int32)
    phase_index = sites[:, None] * wave_index[None, :] % momenta
    angles = phase_index.astype(jnp.float32) * (2.0 * math.pi / momenta)
    return (jnp.cos(angles), jnp.sin(angles))


def forward_matrix(cosine_table, sine_table, momenta):
    return (
        jnp.concatenate(
            [
                jnp.concatenate([cosine_table, -sine_table], 1),
                jnp.concatenate([sine_table, cosine_table], 1),
            ],
            0,
        )
        / momenta
    )


def inverse_matrix(cosine_table, sine_table):
    return jnp.concatenate(
        [
            jnp.concatenate([cosine_table.T, sine_table.T], 1),
            jnp.concatenate([-sine_table.T, cosine_table.T], 1),
        ],
        0,
    )


def cubic_product(site_full, mirror):
    square_re = site_full[0] * site_full[0] - site_full[1] * site_full[1]
    square_im = 2.0 * site_full[0] * site_full[1]
    strength = coupling * coupling
    sigma_re = strength * (square_re * mirror[0] - square_im * mirror[1])
    sigma_im = strength * (square_re * mirror[1] + square_im * mirror[0])
    return jnp.stack([sigma_re, sigma_im])


def general_shards(green_function):
    highest = lax.Precision.HIGHEST
    rows_count = lax.axis_size("tr")
    cols_count = lax.axis_size("tc")
    devices = rows_count * cols_count
    momenta = green_function.shape[1]
    tile_rows = green_function.shape[2]
    tile_cols = green_function.shape[3]
    window = tile_rows * rows_count
    per_device = momenta // devices
    half_slots = per_device // 2
    cells = tile_rows * tile_cols
    ratio = cols_count // rows_count
    green_split = green_function.reshape(2, devices, per_device, cells)
    cosine_table, sine_table = phase_tables(momenta, site_order(momenta, per_device))
    forward = forward_matrix(cosine_table, sine_table, momenta)
    site_tiles = jnp.dot(
        forward, green_function.reshape(2 * momenta, cells), precision=highest
    ).reshape(2, devices, per_device, cells)
    arrived = lax.all_to_all(site_tiles, ("tr", "tc"), split_axis=1, concat_axis=1, tiled=True)
    item_count = arrived.shape[2]
    shaped = arrived.reshape(2, rows_count, cols_count, item_count, tile_rows, tile_cols)
    site_full = shaped.transpose(0, 3, 1, 4, 2, 5).reshape(2, item_count, window, window)
    device = lax.axis_index("tr") * cols_count + lax.axis_index("tc")
    slot_index = jnp.arange(per_device, dtype=jnp.int32)
    self_mirror = (device == 0) & ((slot_index == 0) | (slot_index == half_slots))
    swapped = jnp.concatenate([site_full[:, half_slots:], site_full[:, :half_slots]], 1)
    mirror = jnp.swapaxes(jnp.where(self_mirror[None, :, None, None], site_full, swapped), 2, 3)
    site_sigma = cubic_product(site_full, mirror)
    outgoing = (
        site_sigma.reshape(2, per_device, rows_count, tile_rows, cols_count, tile_cols)
        .transpose(0, 2, 4, 1, 3, 5)
        .reshape(2, devices, per_device, cells)
    )
    returned = lax.all_to_all(outgoing, ("tr", "tc"), split_axis=1, concat_axis=1, tiled=True)
    inverse = inverse_matrix(cosine_table, sine_table)
    sigma_tiles = jnp.dot(inverse, returned.reshape(2 * momenta, cells), precision=highest).reshape(
        2, devices, per_device, cells
    )
    sigma_pieces = lax.all_to_all(
        sigma_tiles, ("tr", "tc"), split_axis=1, concat_axis=1, tiled=True
    )
    item_count = sigma_pieces.shape[2]
    sigma = sigma_pieces.reshape(2, rows_count, rows_count, ratio, item_count, tile_rows, tile_cols)
    green = lax.all_to_all(
        green_split, ("tr", "tc"), split_axis=1, concat_axis=1, tiled=True
    ).reshape(2, rows_count, cols_count, item_count, ratio, tile_cols, tile_cols)
    form = "agjktx,gDkjxu->katDu"
    real_part = jnp.einsum(form, sigma[0], green[0], precision=highest) - jnp.einsum(
        form, sigma[1], green[1], precision=highest
    )
    imag_part = jnp.einsum(form, sigma[0], green[1], precision=highest) + jnp.einsum(
        form, sigma[1], green[0], precision=highest
    )
    stacked = jnp.stack([real_part, imag_part])
    return time_step * stacked.reshape(2, item_count, window, window)


def kept_half(a, b):
    z, c = b // 2, b % 2
    return 1 - c if a < z else c if a > z else 0


def partner(a, b):
    z, c = b // 2, b % 2
    return (z, 2 * a + c) if a < z else (z, 2 * a + 1 - c)


def ways(rows_count):
    return (0, 1, rows_count // 2, rows_count // 2 + 1)


def block_plan(rows_count):
    cols_count = 2 * rows_count
    first = [[] for _ in ways(rows_count)]
    second = [[] for _ in ways(rows_count)]
    held = {}
    for a in range(rows_count):
        for b in range(cols_count):
            source = a * cols_count + b
            pa, pb = partner(a, b)
            target = pa * cols_count + pb
            for n, flip in enumerate(ways(rows_count)):
                middle = (a ^ flip) * cols_count + b
                first[n].append((source, middle))
                second[n].append((middle, target))
            keep = kept_half(a, b)
            held[(2 * a + keep, b)] = (source, 0)
            held[(2 * a + 1 - keep, b)] = (target, 1)
    return first, second, held


def split(x):
    high = x.astype(bf16)
    return high, (x - high.astype(f32)).astype(bf16)


def dot(x, y, dims=((1,), (0,))):
    return lax.dot_general(x, y, (dims, ((), ())), preferred_element_type=f32)


def dot3(x, y, dims=((1,), (0,))):
    return dot(x[0], y[0], dims) + dot(x[0], y[1], dims) + dot(x[1], y[0], dims)


def regroup(x):
    lane = lax.broadcasted_iota(jnp.int32, x[0].shape, 1)
    upper = lane >= LANES // 2
    odd = (lane // (LANES // 4)) % 2 == 1
    half, quarter = LANES // 2, LANES // 4

    def swap(p, q, mask, shift):
        return (
            jnp.where(mask, pltpu.roll(q, shift, 1), p),
            jnp.where(mask, q, pltpu.roll(p, LANES - shift, 1)),
        )

    a0, a2 = swap(x[0], x[2], upper, half)
    a1, a3 = swap(x[1], x[3], upper, half)
    y0, y1 = swap(a0, a1, odd, quarter)
    y2, y3 = swap(a2, a3, odd, quarter)
    return y0, y1, y2, y3


def send_kernel(x_ref, out_ref):
    for v in range(SUBLANES):
        rows = jnp.concatenate([x_ref[0, q, v] for q in range(4)], 0)
        out_ref[:, 0, v] = rows.T.reshape(out_ref.shape[0], SUBLANES, LANES)


def pack_green(x, start, count):
    _, rows, cols, momenta = x.shape
    devices = momenta // SUBLANES
    parts = momenta // LANES
    spans = rows * cols // LANES
    per_part = spans // SUBLANES
    x = x.reshape(2, 4, spans, cols, momenta)
    return pl.pallas_call(
        send_kernel,
        grid=(count, parts),
        in_specs=[
            pl.BlockSpec(
                (1, 4, SUBLANES, cols, LANES),
                lambda n, p: ((n + start) // per_part, 0, (n + start) % per_part, 0, p),
            )
        ],
        out_specs=pl.BlockSpec(
            (devices // parts, 1, SUBLANES, SUBLANES, LANES), lambda n, p: (p, n, 0, 0, 0)
        ),
        out_shape=jax.ShapeDtypeStruct((devices, count, SUBLANES, SUBLANES, LANES), f32),
        cost_estimate=pl.CostEstimate(
            flops=0, bytes_accessed=4 * x.size * count // per_part, transcendentals=0
        ),
        name="pack_green",
    )(x)


def sigma_kernel(flags, kept_ref, re0_ref, re1_ref, im0_ref, im1_ref, fh_ref, fl_ref, ih_ref, il_ref, out_ref, plus, minus):
    points, momenta = kept_ref.shape[2], kept_ref.shape[3]
    edge = math.isqrt(points)
    spans = points // LANES
    chunk = 256
    forward = (fh_ref[...], fl_ref[...])

    half = points // 2
    pieces = (
        (0, 0, points, kept_ref.at[0, 0], kept_ref.at[1, 0]),
        (1, 0, half, re0_ref, im0_ref),
        (1, half, half, re1_ref, im1_ref),
    )
    for unit, start, count, re_ref, im_ref in pieces:

        def transform(n, carry, unit=unit, start=start, re_ref=re_ref, im_ref=im_ref):
            source = pl.ds(pl.multiple_of(n * chunk, chunk), chunk)
            rows = pl.ds(pl.multiple_of(start + n * chunk, chunk), chunk)
            y_re = dot3(split(re_ref[source, :]), forward)
            y_im = dot3(split(im_ref[source, :]), forward)
            re_c, re_s = y_re[:, :momenta], y_re[:, momenta:]
            im_c, im_s = y_im[:, :momenta], y_im[:, momenta:]
            plus[unit, 0, rows, :] = re_c - im_s
            plus[unit, 1, rows, :] = re_s + im_c
            m_re = re_c + im_s
            m_im = im_c - re_s
            for p in range(momenta // LANES):
                lanes = slice(LANES * p, LANES * (p + 1))
                minus[unit, 0, p, rows, :] = m_re[:, lanes]
                minus[unit, 1, p, rows, :] = m_im[:, lanes]
            return carry

        lax.fori_loop(0, count // chunk, transform, 0)

    inverse = (ih_ref[...], il_ref[...])
    diagonal = flags[1]
    for unit in range(2):
        facing = jnp.where(diagonal == 1, unit, 1 - unit)

        def combine(n, carry, unit=unit, facing=facing):
            s_re, s_im = [], []
            for w in range(2):
                for q in range(4):
                    i = spans * q + 2 * n + w
                    rows = pl.ds(pl.multiple_of(i * edge, edge), edge)
                    across = pl.ds(i, edge, stride=edge)
                    p_re, p_im = plus[unit, 0, rows, :], plus[unit, 1, rows, :]
                    m_re, m_im = (
                        jnp.concatenate(
                            [minus[facing, c, p, across, :] for p in range(momenta // LANES)], 1
                        )
                        for c in range(2)
                    )
                    sq_re = p_re * p_re - p_im * p_im
                    sq_im = 2.0 * p_re * p_im
                    s_re.append(sq_re * m_re - sq_im * m_im)
                    s_im.append(sq_re * m_im + sq_im * m_re)
            nt = ((1,), (1,))
            t_re = dot3(inverse, split(jnp.concatenate(s_re, 0)), nt)
            t_im = dot3(inverse, split(jnp.concatenate(s_im, 0)), nt)
            o_re = t_re[:momenta] + t_im[momenta:]
            o_im = t_im[:momenta] - t_re[momenta:]
            for w in range(2):
                lanes = slice(LANES * w, LANES * (w + 1))
                place = spans * unit + 2 * n + w
                shape = (momenta // SUBLANES, SUBLANES, LANES)
                out_ref[:, 0, place] = o_re[:, lanes].reshape(shape)
                out_ref[:, 1, place] = o_im[:, lanes].reshape(shape)
            return carry

        lax.fori_loop(0, spans // 2, combine, 0)


def form_sigma(flags, x, others, tables):
    comps, _, points, momenta = x.shape
    devices = momenta // SUBLANES
    spans = 2 * points // LANES
    whole = lambda a: pl.BlockSpec(a.shape, lambda n, s: (0,) * a.ndim)
    flops = 3 * 2 * 4 * 2 * (2 * points) * momenta * momenta
    return pl.pallas_call(
        sigma_kernel,
        grid_spec=pltpu.PrefetchScalarGridSpec(
            num_scalar_prefetch=1,
            grid=(1,),
            in_specs=[
                pl.BlockSpec((comps, 1, points, momenta), lambda n, s: (0, s[0], 0, 0)),
                *[whole(t) for t in others],
                *[whole(t) for t in tables],
            ],
            out_specs=pl.BlockSpec(
                (devices, comps, spans, SUBLANES, LANES), lambda n, s: (0, 0, 0, 0, 0)
            ),
            scratch_shapes=[
                pltpu.VMEM((2, comps, points, momenta), f32),
                pltpu.VMEM((2, comps, momenta // LANES, points, LANES), f32),
            ],
        ),
        out_shape=jax.ShapeDtypeStruct((devices, comps, spans, SUBLANES, LANES), f32),
        cost_estimate=pl.CostEstimate(
            flops=flops, bytes_accessed=12 * others[0].size * 4, transcendentals=0
        ),
        compiler_params=pltpu.CompilerParams(vmem_limit_bytes=56 * 1024 * 1024),
        name="form_sigma",
    )(flags, x, *others, *tables)


def green_kernel(first_ref, rest_ref, out_ref, *, rows_count):
    cols_count = 2 * rows_count
    k = pl.program_id(0)
    tile_rows = out_ref.shape[3] // rows_count
    step = tile_rows // 4
    parts = step // SUBLANES
    refs = [first_ref.at[:, n] for n in range(first_ref.shape[1])]
    refs += [rest_ref.at[:, n] for n in range(rest_ref.shape[1])]
    for comp in range(2):
        for a in range(rows_count):
            for side in range(cols_count // 4):
                groups = [[] for _ in range(4)]
                for part in range(parts):
                    x_ref = refs[parts * comp + part]
                    span = pl.ds(k, SUBLANES, stride=SUBLANES)
                    loaded = [x_ref[a * cols_count + 4 * side + n, span, :] for n in range(4)]
                    for q, value in enumerate(regroup(loaded)):
                        groups[q].append(value)
                for q in range(4):
                    high, low = split(jnp.concatenate(groups[q], 0))
                    rows = slice(tile_rows * a + step * q, tile_rows * a + step * (q + 1))
                    lanes = slice(LANES * side, LANES * (side + 1))
                    out_ref[0, comp, 0, rows, lanes] = high
                    out_ref[0, comp, 1, rows, lanes] = low


def arrange_green(parts, rows_count, window):
    parts = [x.reshape(*x.shape[:2], SUBLANES * SUBLANES, LANES) for x in parts]
    return pl.pallas_call(
        functools.partial(green_kernel, rows_count=rows_count),
        grid=(SUBLANES,),
        in_specs=[pl.BlockSpec(x.shape, lambda k: (0, 0, 0, 0)) for x in parts],
        out_specs=pl.BlockSpec((1, 2, 2, window, window), lambda k: (k, 0, 0, 0, 0)),
        out_shape=jax.ShapeDtypeStruct((SUBLANES, 2, 2, window, window), bf16),
        cost_estimate=pl.CostEstimate(
            flops=0, bytes_accessed=8 * sum(x.size for x in parts), transcendentals=0
        ),
        name="arrange_green",
    )(*parts)


def collide_kernel(s_ref, g_ref, out_ref, left, *, held, blocks):
    k = pl.program_id(0)
    edge = out_ref.shape[2] // blocks
    for comp in range(2):
        for row in range(blocks):
            for side in range(blocks // 4):
                loaded = []
                for n in range(4):
                    source, unit = held[(row, 4 * side + n)]
                    span = pl.ds(SUBLANES * SUBLANES * unit + k, SUBLANES, stride=SUBLANES)
                    loaded.append(s_ref[source, comp, span, :])
                high, low = split(jnp.concatenate(regroup(loaded), 0))
                rows = slice(edge * row, edge * (row + 1))
                lanes = slice(LANES * side, LANES * (side + 1))
                left[comp, 0, rows, lanes] = high
                left[comp, 1, rows, lanes] = low
    re, im = ((left[c, 0], left[c, 1]) for c in range(2))
    g_re, g_im = ((g_ref[0, c, 0], g_ref[0, c, 1]) for c in range(2))
    out_ref[0, 0] = time_step * (dot3(re, g_re) - dot3(im, g_im))
    out_ref[1, 0] = time_step * (dot3(re, g_im) + dot3(im, g_re))


def collide(sigma, green, held, blocks):
    window = green.shape[-1]
    sigma = sigma.reshape(sigma.shape[0], 2, -1, LANES)
    return pl.pallas_call(
        functools.partial(collide_kernel, held=held, blocks=blocks),
        grid=(SUBLANES,),
        in_specs=[
            pl.BlockSpec(sigma.shape, lambda k: (0, 0, 0, 0)),
            pl.BlockSpec((1, 2, 2, window, window), lambda k: (k, 0, 0, 0, 0)),
        ],
        out_specs=pl.BlockSpec((2, 1, window, window), lambda k: (0, k, 0, 0)),
        out_shape=jax.ShapeDtypeStruct((2, SUBLANES, window, window), f32),
        scratch_shapes=[pltpu.VMEM((2, 2, window, window), bf16)],
        cost_estimate=pl.CostEstimate(
            flops=3 * 8 * SUBLANES * window**3, bytes_accessed=3 * sigma.size * 4, transcendentals=0
        ),
        name="collide",
    )(sigma, green)


def table_pair(values):
    high = values.astype(np.float32).astype(bf16)
    low = (values - high.astype(np.float64)).astype(np.float32).astype(bf16)
    return jnp.asarray(high), jnp.asarray(low)


def dft_tables(momenta):
    index = np.arange(momenta)
    angle = 2.0 * np.pi * (index[:, None] * index[None, :] % momenta) / momenta
    cosine, sine = np.cos(angle), np.sin(angle)
    strength = coupling * coupling / momenta**3
    forward = np.concatenate([cosine, sine], 1)
    inverse = strength * np.concatenate([cosine, sine], 0)
    return (*table_pair(forward), *table_pair(inverse))


def packed_shards(green_function):
    axes = ("tr", "tc")
    rows_count = lax.axis_size("tr")
    comps, momenta, tile_rows, tile_cols = green_function.shape
    window = tile_rows * rows_count
    points = tile_cols * tile_cols
    first, second, held = block_plan(rows_count)
    a = lax.axis_index("tr")
    b = lax.axis_index("tc")
    z, c = b // 2, b % 2
    keep = jnp.where(a < z, 1 - c, jnp.where(a > z, c, 0)).astype(jnp.int32)
    diagonal = ((a == z) & (c == 0)).astype(jnp.int32)

    x = green_function.transpose(0, 2, 3, 1)
    halves = x.reshape(comps, 2, points, momenta)
    half = points // 2
    leaving = [
        lax.dynamic_slice(
            halves, (n // 2, 1 - keep, half * (n % 2), 0), (1, 1, half, momenta)
        ).reshape(half, momenta)
        for n in range(4)
    ]
    tables = dft_tables(momenta)
    others = list(leaving)
    for n in range(1, 4):
        others[n] = lax.ppermute(others[n], axes, first[n])
    for n in range(4):
        others[n] = lax.ppermute(others[n], axes, second[n])
    pieces = comps * tile_rows * tile_cols // (SUBLANES * LANES)
    early = pieces // 4
    green = [pack_green(x, 0, early), pack_green(x, early, pieces - early)]
    for n in range(2):
        green[n] = lax.all_to_all(green[n], axes, split_axis=0, concat_axis=0, tiled=True)
    sigma = form_sigma(jnp.stack([keep, diagonal]), halves, others, tables)
    sigma = lax.all_to_all(sigma, axes, split_axis=0, concat_axis=0, tiled=True)
    green = arrange_green(green, rows_count, window)
    return collide(sigma, green, held, 2 * rows_count)


def is_packed(rows_count, cols_count, comps, momenta, tile_rows, tile_cols):
    return (
        cols_count == 2 * rows_count
        and tile_rows == 2 * tile_cols
        and 4 * tile_cols == LANES
        and momenta == SUBLANES * rows_count * cols_count
        and momenta % LANES == 0
        and cols_count % 4 == 0
        and rows_count & (rows_count - 1) == 0
    )


def shards(green_function):
    sizes = (lax.axis_size("tr"), lax.axis_size("tc"), *green_function.shape)
    return packed_shards(green_function) if is_packed(*sizes) else general_shards(green_function)


def solution(mesh):
    return jax.shard_map(
        shards,
        mesh=mesh,
        in_specs=(P(None, None, "tr", "tc"),),
        out_specs=P(None, ("tr", "tc"), None, None),
        check_vma=False,
    )
```

```python
import functools
import math

import jax
import jax.numpy as jnp
import numpy as np
from jax import lax
from jax.experimental import pallas as pl
from jax.experimental.pallas import tpu as pltpu
from jax.sharding import PartitionSpec as P

coupling = 4.0
time_step = 0.2
f32 = jnp.float32
bf16 = jnp.bfloat16
LANES = 128
SUBLANES = 8


def site_order(momenta, per_device):
    positions = jnp.arange(momenta, dtype=jnp.int32)
    half_slots = per_device // 2
    owner_index = positions // per_device
    slot_in_device = positions % per_device
    base_site = owner_index * half_slots + slot_in_device % half_slots
    mirrored = jnp.where(base_site == 0, momenta // 2, momenta - base_site)
    return jnp.where(slot_in_device < half_slots, base_site, mirrored)


def phase_tables(momenta, sites):
    wave_index = jnp.arange(momenta, dtype=jnp.int32)
    phase_index = sites[:, None] * wave_index[None, :] % momenta
    angles = phase_index.astype(jnp.float32) * (2.0 * math.pi / momenta)
    return (jnp.cos(angles), jnp.sin(angles))


def forward_matrix(cosine_table, sine_table, momenta):
    return (
        jnp.concatenate(
            [
                jnp.concatenate([cosine_table, -sine_table], 1),
                jnp.concatenate([sine_table, cosine_table], 1),
            ],
            0,
        )
        / momenta
    )


def inverse_matrix(cosine_table, sine_table):
    return jnp.concatenate(
        [
            jnp.concatenate([cosine_table.T, sine_table.T], 1),
            jnp.concatenate([-sine_table.T, cosine_table.T], 1),
        ],
        0,
    )


def cubic_product(site_full, mirror):
    square_re = site_full[0] * site_full[0] - site_full[1] * site_full[1]
    square_im = 2.0 * site_full[0] * site_full[1]
    strength = coupling * coupling
    sigma_re = strength * (square_re * mirror[0] - square_im * mirror[1])
    sigma_im = strength * (square_re * mirror[1] + square_im * mirror[0])
    return jnp.stack([sigma_re, sigma_im])


def general_shards(green_function):
    highest = lax.Precision.HIGHEST
    rows_count = lax.axis_size("tr")
    cols_count = lax.axis_size("tc")
    devices = rows_count * cols_count
    momenta = green_function.shape[1]
    tile_rows = green_function.shape[2]
    tile_cols = green_function.shape[3]
    window = tile_rows * rows_count
    per_device = momenta // devices
    half_slots = per_device // 2
    cells = tile_rows * tile_cols
    ratio = cols_count // rows_count
    green_split = green_function.reshape(2, devices, per_device, cells)
    cosine_table, sine_table = phase_tables(momenta, site_order(momenta, per_device))
    forward = forward_matrix(cosine_table, sine_table, momenta)
    site_tiles = jnp.dot(
        forward, green_function.reshape(2 * momenta, cells), precision=highest
    ).reshape(2, devices, per_device, cells)
    arrived = lax.all_to_all(site_tiles, ("tr", "tc"), split_axis=1, concat_axis=1, tiled=True)
    item_count = arrived.shape[2]
    shaped = arrived.reshape(2, rows_count, cols_count, item_count, tile_rows, tile_cols)
    site_full = shaped.transpose(0, 3, 1, 4, 2, 5).reshape(2, item_count, window, window)
    device = lax.axis_index("tr") * cols_count + lax.axis_index("tc")
    slot_index = jnp.arange(per_device, dtype=jnp.int32)
    self_mirror = (device == 0) & ((slot_index == 0) | (slot_index == half_slots))
    swapped = jnp.concatenate([site_full[:, half_slots:], site_full[:, :half_slots]], 1)
    mirror = jnp.swapaxes(jnp.where(self_mirror[None, :, None, None], site_full, swapped), 2, 3)
    site_sigma = cubic_product(site_full, mirror)
    outgoing = (
        site_sigma.reshape(2, per_device, rows_count, tile_rows, cols_count, tile_cols)
        .transpose(0, 2, 4, 1, 3, 5)
        .reshape(2, devices, per_device, cells)
    )
    returned = lax.all_to_all(outgoing, ("tr", "tc"), split_axis=1, concat_axis=1, tiled=True)
    inverse = inverse_matrix(cosine_table, sine_table)
    sigma_tiles = jnp.dot(inverse, returned.reshape(2 * momenta, cells), precision=highest).reshape(
        2, devices, per_device, cells
    )
    sigma_pieces = lax.all_to_all(
        sigma_tiles, ("tr", "tc"), split_axis=1, concat_axis=1, tiled=True
    )
    item_count = sigma_pieces.shape[2]
    sigma = sigma_pieces.reshape(2, rows_count, rows_count, ratio, item_count, tile_rows, tile_cols)
    green = lax.all_to_all(
        green_split, ("tr", "tc"), split_axis=1, concat_axis=1, tiled=True
    ).reshape(2, rows_count, cols_count, item_count, ratio, tile_cols, tile_cols)
    form = "agjktx,gDkjxu->katDu"
    real_part = jnp.einsum(form, sigma[0], green[0], precision=highest) - jnp.einsum(
        form, sigma[1], green[1], precision=highest
    )
    imag_part = jnp.einsum(form, sigma[0], green[1], precision=highest) + jnp.einsum(
        form, sigma[1], green[0], precision=highest
    )
    stacked = jnp.stack([real_part, imag_part])
    return time_step * stacked.reshape(2, item_count, window, window)


def kept_half(a, b):
    z, c = b // 2, b % 2
    return 1 - c if a < z else c if a > z else 0


def partner(a, b):
    z, c = b // 2, b % 2
    return (z, 2 * a + c) if a < z else (z, 2 * a + 1 - c)


def ways(rows_count):
    return (0, 1, rows_count // 2, rows_count // 2 + 1)


def block_plan(rows_count):
    cols_count = 2 * rows_count
    first = [[] for _ in ways(rows_count)]
    second = [[] for _ in ways(rows_count)]
    held = {}
    for a in range(rows_count):
        for b in range(cols_count):
            source = a * cols_count + b
            pa, pb = partner(a, b)
            target = pa * cols_count + pb
            for n, flip in enumerate(ways(rows_count)):
                middle = (a ^ flip) * cols_count + b
                first[n].append((source, middle))
                second[n].append((middle, target))
            keep = kept_half(a, b)
            held[(2 * a + keep, b)] = (source, 0)
            held[(2 * a + 1 - keep, b)] = (target, 1)
    return first, second, held


def split(x):
    high = x.astype(bf16)
    return high, (x - high.astype(f32)).astype(bf16)


def dot(x, y, dims=((1,), (0,))):
    return lax.dot_general(x, y, (dims, ((), ())), preferred_element_type=f32)


def dot3(x, y, dims=((1,), (0,))):
    return dot(x[0], y[0], dims) + dot(x[0], y[1], dims) + dot(x[1], y[0], dims)


def regroup(x):
    lane = lax.broadcasted_iota(jnp.int32, x[0].shape, 1)
    upper = lane >= LANES // 2
    odd = (lane // (LANES // 4)) % 2 == 1
    half, quarter = LANES // 2, LANES // 4

    def swap(p, q, mask, shift):
        return (
            jnp.where(mask, pltpu.roll(q, shift, 1), p),
            jnp.where(mask, q, pltpu.roll(p, LANES - shift, 1)),
        )

    a0, a2 = swap(x[0], x[2], upper, half)
    a1, a3 = swap(x[1], x[3], upper, half)
    y0, y1 = swap(a0, a1, odd, quarter)
    y2, y3 = swap(a2, a3, odd, quarter)
    return y0, y1, y2, y3


def send_kernel(x_ref, out_ref):
    spans = out_ref.shape[1]
    for v in range(spans):
        rows = jnp.concatenate([x_ref[0, spans * q + v] for q in range(4)], 0)
        out_ref[:, v] = rows.T.reshape(out_ref.shape[0], SUBLANES, LANES)


def pack_green(x, comp):
    _, rows, cols, momenta = x.shape
    spans = rows * cols // LANES
    devices = momenta // SUBLANES
    parts = momenta // LANES
    return pl.pallas_call(
        send_kernel,
        grid=(parts,),
        in_specs=[pl.BlockSpec((1, rows, cols, LANES), lambda p: (comp, 0, 0, p))],
        out_specs=pl.BlockSpec((devices // parts, spans, SUBLANES, LANES), lambda p: (p, 0, 0, 0)),
        out_shape=jax.ShapeDtypeStruct((devices, spans, SUBLANES, LANES), f32),
        cost_estimate=pl.CostEstimate(flops=0, bytes_accessed=x.size * 4, transcendentals=0),
        name="pack_green",
    )(x)


def sigma_kernel(flags, kept_ref, re0_ref, re1_ref, im0_ref, im1_ref, fh_ref, fl_ref, ih_ref, il_ref, out_ref, plus, minus):
    points, momenta = kept_ref.shape[2], kept_ref.shape[3]
    edge = math.isqrt(points)
    spans = points // LANES
    chunk = 256
    forward = (fh_ref[...], fl_ref[...])

    half = points // 2
    pieces = (
        (0, 0, points, kept_ref.at[0, 0], kept_ref.at[1, 0]),
        (1, 0, half, re0_ref, im0_ref),
        (1, half, half, re1_ref, im1_ref),
    )
    for unit, start, count, re_ref, im_ref in pieces:

        def transform(n, carry, unit=unit, start=start, re_ref=re_ref, im_ref=im_ref):
            source = pl.ds(pl.multiple_of(n * chunk, chunk), chunk)
            rows = pl.ds(pl.multiple_of(start + n * chunk, chunk), chunk)
            y_re = dot3(split(re_ref[source, :]), forward)
            y_im = dot3(split(im_ref[source, :]), forward)
            re_c, re_s = y_re[:, :momenta], y_re[:, momenta:]
            im_c, im_s = y_im[:, :momenta], y_im[:, momenta:]
            plus[unit, 0, rows, :] = re_c - im_s
            plus[unit, 1, rows, :] = re_s + im_c
            m_re = re_c + im_s
            m_im = im_c - re_s
            for p in range(momenta // LANES):
                lanes = slice(LANES * p, LANES * (p + 1))
                minus[unit, 0, p, rows, :] = m_re[:, lanes]
                minus[unit, 1, p, rows, :] = m_im[:, lanes]
            return carry

        lax.fori_loop(0, count // chunk, transform, 0)

    inverse = (ih_ref[...], il_ref[...])
    diagonal = flags[1]
    for unit in range(2):
        facing = jnp.where(diagonal == 1, unit, 1 - unit)

        def combine(n, carry, unit=unit, facing=facing):
            s_re, s_im = [], []
            for w in range(2):
                for q in range(4):
                    i = spans * q + 2 * n + w
                    rows = pl.ds(pl.multiple_of(i * edge, edge), edge)
                    across = pl.ds(i, edge, stride=edge)
                    p_re, p_im = plus[unit, 0, rows, :], plus[unit, 1, rows, :]
                    m_re, m_im = (
                        jnp.concatenate(
                            [minus[facing, c, p, across, :] for p in range(momenta // LANES)], 1
                        )
                        for c in range(2)
                    )
                    sq_re = p_re * p_re - p_im * p_im
                    sq_im = 2.0 * p_re * p_im
                    s_re.append(sq_re * m_re - sq_im * m_im)
                    s_im.append(sq_re * m_im + sq_im * m_re)
            nt = ((1,), (1,))
            t_re = dot3(inverse, split(jnp.concatenate(s_re, 0)), nt)
            t_im = dot3(inverse, split(jnp.concatenate(s_im, 0)), nt)
            o_re = t_re[:momenta] + t_im[momenta:]
            o_im = t_im[:momenta] - t_re[momenta:]
            for w in range(2):
                lanes = slice(LANES * w, LANES * (w + 1))
                place = pl.ds(2 * n + w, SUBLANES, stride=spans)
                shape = (momenta // SUBLANES, SUBLANES, LANES)
                out_ref[:, 0, unit, place, :] = o_re[:, lanes].reshape(shape)
                out_ref[:, 1, unit, place, :] = o_im[:, lanes].reshape(shape)
            return carry

        lax.fori_loop(0, spans // 2, combine, 0)


def form_sigma(flags, x, others, tables):
    comps, _, points, momenta = x.shape
    devices = momenta // SUBLANES
    out_shape = (devices, comps, 2, SUBLANES * points // LANES, LANES)
    whole = lambda a: pl.BlockSpec(a.shape, lambda n, s: (0,) * a.ndim)
    flops = 3 * 2 * 4 * 2 * (2 * points) * momenta * momenta
    return pl.pallas_call(
        sigma_kernel,
        grid_spec=pltpu.PrefetchScalarGridSpec(
            num_scalar_prefetch=1,
            grid=(1,),
            in_specs=[
                pl.BlockSpec((comps, 1, points, momenta), lambda n, s: (0, s[0], 0, 0)),
                *[whole(t) for t in others],
                *[whole(t) for t in tables],
            ],
            out_specs=pl.BlockSpec(out_shape, lambda n, s: (0, 0, 0, 0, 0)),
            scratch_shapes=[
                pltpu.VMEM((2, comps, points, momenta), f32),
                pltpu.VMEM((2, comps, momenta // LANES, points, LANES), f32),
            ],
        ),
        out_shape=jax.ShapeDtypeStruct(out_shape, f32),
        cost_estimate=pl.CostEstimate(
            flops=flops, bytes_accessed=12 * others[0].size * 4, transcendentals=0
        ),
        compiler_params=pltpu.CompilerParams(vmem_limit_bytes=56 * 1024 * 1024),
        name="form_sigma",
    )(flags, x, *others, *tables)


def green_kernel(re_ref, im_ref, out_ref, *, rows_count):
    cols_count = 2 * rows_count
    k = pl.program_id(0)
    tile_rows = out_ref.shape[3] // rows_count
    step = tile_rows // 4
    for comp, x_ref in enumerate((re_ref, im_ref)):
        for a in range(rows_count):
            for side in range(cols_count // 4):
                groups = [[] for _ in range(4)]
                for part in range(step // SUBLANES):
                    span = pl.ds(SUBLANES * SUBLANES * part + k, SUBLANES, stride=SUBLANES)
                    loaded = [
                        x_ref[a * cols_count + 4 * side + n, span, :] for n in range(4)
                    ]
                    for q, value in enumerate(regroup(loaded)):
                        groups[q].append(value)
                for q in range(4):
                    high, low = split(jnp.concatenate(groups[q], 0))
                    rows = slice(tile_rows * a + step * q, tile_rows * a + step * (q + 1))
                    lanes = slice(LANES * side, LANES * (side + 1))
                    out_ref[0, comp, 0, rows, lanes] = high
                    out_ref[0, comp, 1, rows, lanes] = low


def arrange_green(parts, rows_count, window):
    parts = [x.reshape(x.shape[0], -1, LANES) for x in parts]
    return pl.pallas_call(
        functools.partial(green_kernel, rows_count=rows_count),
        grid=(SUBLANES,),
        in_specs=[pl.BlockSpec(x.shape, lambda k: (0, 0, 0)) for x in parts],
        out_specs=pl.BlockSpec((1, 2, 2, window, window), lambda k: (k, 0, 0, 0, 0)),
        out_shape=jax.ShapeDtypeStruct((SUBLANES, 2, 2, window, window), bf16),
        cost_estimate=pl.CostEstimate(
            flops=0, bytes_accessed=4 * parts[0].size * 4, transcendentals=0
        ),
        name="arrange_green",
    )(*parts)


def collide_kernel(s_ref, g_ref, out_ref, left, *, held, blocks):
    window = out_ref.shape[2]
    edge = window // blocks
    for comp in range(2):
        for row in range(blocks):
            for side in range(blocks // 4):
                loaded = []
                for n in range(4):
                    source, unit = held[(row, 4 * side + n)]
                    loaded.append(s_ref[source, comp, unit, 0])
                high, low = split(jnp.concatenate(regroup(loaded), 0))
                rows = slice(edge * row, edge * (row + 1))
                lanes = slice(LANES * side, LANES * (side + 1))
                left[comp, 0, rows, lanes] = high
                left[comp, 1, rows, lanes] = low
    re, im = ((left[c, 0], left[c, 1]) for c in range(2))
    g_re, g_im = ((g_ref[0, c, 0], g_ref[0, c, 1]) for c in range(2))
    out_ref[0, 0] = time_step * (dot3(re, g_re) - dot3(im, g_im))
    out_ref[1, 0] = time_step * (dot3(re, g_im) + dot3(im, g_re))


def collide(sigma, green, held, blocks):
    window = green.shape[-1]
    rows = sigma.shape[3] // SUBLANES
    sigma = sigma.reshape(*sigma.shape[:3], SUBLANES, rows, LANES)
    return pl.pallas_call(
        functools.partial(collide_kernel, held=held, blocks=blocks),
        grid=(SUBLANES,),
        in_specs=[
            pl.BlockSpec((*sigma.shape[:3], 1, rows, LANES), lambda k: (0, 0, 0, k, 0, 0)),
            pl.BlockSpec((1, 2, 2, window, window), lambda k: (k, 0, 0, 0, 0)),
        ],
        out_specs=pl.BlockSpec((2, 1, window, window), lambda k: (0, k, 0, 0)),
        out_shape=jax.ShapeDtypeStruct((2, SUBLANES, window, window), f32),
        scratch_shapes=[pltpu.VMEM((2, 2, window, window), bf16)],
        cost_estimate=pl.CostEstimate(
            flops=3 * 8 * SUBLANES * window**3, bytes_accessed=3 * sigma.size * 4, transcendentals=0
        ),
        name="collide",
    )(sigma, green)


def table_pair(values):
    high = values.astype(np.float32).astype(bf16)
    low = (values - high.astype(np.float64)).astype(np.float32).astype(bf16)
    return jnp.asarray(high), jnp.asarray(low)


def dft_tables(momenta):
    index = np.arange(momenta)
    angle = 2.0 * np.pi * (index[:, None] * index[None, :] % momenta) / momenta
    cosine, sine = np.cos(angle), np.sin(angle)
    strength = coupling * coupling / momenta**3
    forward = np.concatenate([cosine, sine], 1)
    inverse = strength * np.concatenate([cosine, sine], 0)
    return (*table_pair(forward), *table_pair(inverse))


def packed_shards(green_function):
    axes = ("tr", "tc")
    rows_count = lax.axis_size("tr")
    comps, momenta, tile_rows, tile_cols = green_function.shape
    window = tile_rows * rows_count
    points = tile_cols * tile_cols
    first, second, held = block_plan(rows_count)
    a = lax.axis_index("tr")
    b = lax.axis_index("tc")
    z, c = b // 2, b % 2
    keep = jnp.where(a < z, 1 - c, jnp.where(a > z, c, 0)).astype(jnp.int32)
    diagonal = ((a == z) & (c == 0)).astype(jnp.int32)

    x = green_function.transpose(0, 2, 3, 1)
    halves = x.reshape(comps, 2, points, momenta)
    half = points // 2
    leaving = [
        lax.dynamic_slice(
            halves, (n // 2, 1 - keep, half * (n % 2), 0), (1, 1, half, momenta)
        ).reshape(half, momenta)
        for n in range(4)
    ]
    tables = dft_tables(momenta)
    others = list(leaving)
    for n in range(1, 4):
        others[n] = lax.ppermute(others[n], axes, first[n])
    for n in range(4):
        others[n] = lax.ppermute(others[n], axes, second[n])
    green = [pack_green(x, comp) for comp in range(comps)]
    for comp in range(comps):
        green[comp] = lax.all_to_all(green[comp], axes, split_axis=0, concat_axis=0, tiled=True)
    sigma = form_sigma(jnp.stack([keep, diagonal]), halves, others, tables)
    sigma = lax.all_to_all(sigma, axes, split_axis=0, concat_axis=0, tiled=True)
    green = arrange_green(green, rows_count, window)
    return collide(sigma, green, held, 2 * rows_count)


def is_packed(rows_count, cols_count, comps, momenta, tile_rows, tile_cols):
    return (
        cols_count == 2 * rows_count
        and tile_rows == 2 * tile_cols
        and 4 * tile_cols == LANES
        and momenta == SUBLANES * rows_count * cols_count
        and momenta % LANES == 0
        and cols_count % 4 == 0
        and rows_count & (rows_count - 1) == 0
    )


def shards(green_function):
    sizes = (lax.axis_size("tr"), lax.axis_size("tc"), *green_function.shape)
    return packed_shards(green_function) if is_packed(*sizes) else general_shards(green_function)


def solution(mesh):
    return jax.shard_map(
        shards,
        mesh=mesh,
        in_specs=(P(None, None, "tr", "tc"),),
        out_specs=P(None, ("tr", "tc"), None, None),
        check_vma=False,
    )
```

```python
import functools
import math

import jax
import jax.numpy as jnp
import numpy as np
from jax import lax
from jax.experimental import pallas as pl
from jax.experimental.pallas import tpu as pltpu
from jax.sharding import PartitionSpec as P

coupling = 4.0
time_step = 0.2
f32 = jnp.float32
bf16 = jnp.bfloat16
LANES = 128
GROUP = 4
SUBLANES = 8


def site_order(momenta, per_device):
    positions = jnp.arange(momenta, dtype=jnp.int32)
    half_slots = per_device // 2
    owner_index = positions // per_device
    slot_in_device = positions % per_device
    base_site = owner_index * half_slots + slot_in_device % half_slots
    mirrored = jnp.where(base_site == 0, momenta // 2, momenta - base_site)
    return jnp.where(slot_in_device < half_slots, base_site, mirrored)


def phase_tables(momenta, sites):
    wave_index = jnp.arange(momenta, dtype=jnp.int32)
    phase_index = sites[:, None] * wave_index[None, :] % momenta
    angles = phase_index.astype(jnp.float32) * (2.0 * math.pi / momenta)
    return (jnp.cos(angles), jnp.sin(angles))


def forward_matrix(cosine_table, sine_table, momenta):
    return (
        jnp.concatenate(
            [
                jnp.concatenate([cosine_table, -sine_table], 1),
                jnp.concatenate([sine_table, cosine_table], 1),
            ],
            0,
        )
        / momenta
    )


def inverse_matrix(cosine_table, sine_table):
    return jnp.concatenate(
        [
            jnp.concatenate([cosine_table.T, sine_table.T], 1),
            jnp.concatenate([-sine_table.T, cosine_table.T], 1),
        ],
        0,
    )


def cubic_product(site_full, mirror):
    square_re = site_full[0] * site_full[0] - site_full[1] * site_full[1]
    square_im = 2.0 * site_full[0] * site_full[1]
    strength = coupling * coupling
    sigma_re = strength * (square_re * mirror[0] - square_im * mirror[1])
    sigma_im = strength * (square_re * mirror[1] + square_im * mirror[0])
    return jnp.stack([sigma_re, sigma_im])


def general_shards(green_function):
    highest = lax.Precision.HIGHEST
    rows_count = lax.axis_size("tr")
    cols_count = lax.axis_size("tc")
    devices = rows_count * cols_count
    momenta = green_function.shape[1]
    tile_rows = green_function.shape[2]
    tile_cols = green_function.shape[3]
    window = tile_rows * rows_count
    per_device = momenta // devices
    half_slots = per_device // 2
    cells = tile_rows * tile_cols
    ratio = cols_count // rows_count
    green_split = green_function.reshape(2, devices, per_device, cells)
    cosine_table, sine_table = phase_tables(momenta, site_order(momenta, per_device))
    forward = forward_matrix(cosine_table, sine_table, momenta)
    site_tiles = jnp.dot(
        forward, green_function.reshape(2 * momenta, cells), precision=highest
    ).reshape(2, devices, per_device, cells)
    arrived = lax.all_to_all(site_tiles, ("tr", "tc"), split_axis=1, concat_axis=1, tiled=True)
    item_count = arrived.shape[2]
    shaped = arrived.reshape(2, rows_count, cols_count, item_count, tile_rows, tile_cols)
    site_full = shaped.transpose(0, 3, 1, 4, 2, 5).reshape(2, item_count, window, window)
    device = lax.axis_index("tr") * cols_count + lax.axis_index("tc")
    slot_index = jnp.arange(per_device, dtype=jnp.int32)
    self_mirror = (device == 0) & ((slot_index == 0) | (slot_index == half_slots))
    swapped = jnp.concatenate([site_full[:, half_slots:], site_full[:, :half_slots]], 1)
    mirror = jnp.swapaxes(jnp.where(self_mirror[None, :, None, None], site_full, swapped), 2, 3)
    site_sigma = cubic_product(site_full, mirror)
    outgoing = (
        site_sigma.reshape(2, per_device, rows_count, tile_rows, cols_count, tile_cols)
        .transpose(0, 2, 4, 1, 3, 5)
        .reshape(2, devices, per_device, cells)
    )
    returned = lax.all_to_all(outgoing, ("tr", "tc"), split_axis=1, concat_axis=1, tiled=True)
    inverse = inverse_matrix(cosine_table, sine_table)
    sigma_tiles = jnp.dot(inverse, returned.reshape(2 * momenta, cells), precision=highest).reshape(
        2, devices, per_device, cells
    )
    sigma_pieces = lax.all_to_all(
        sigma_tiles, ("tr", "tc"), split_axis=1, concat_axis=1, tiled=True
    )
    item_count = sigma_pieces.shape[2]
    sigma = sigma_pieces.reshape(2, rows_count, rows_count, ratio, item_count, tile_rows, tile_cols)
    green = lax.all_to_all(
        green_split, ("tr", "tc"), split_axis=1, concat_axis=1, tiled=True
    ).reshape(2, rows_count, cols_count, item_count, ratio, tile_cols, tile_cols)
    form = "agjktx,gDkjxu->katDu"
    real_part = jnp.einsum(form, sigma[0], green[0], precision=highest) - jnp.einsum(
        form, sigma[1], green[1], precision=highest
    )
    imag_part = jnp.einsum(form, sigma[0], green[1], precision=highest) + jnp.einsum(
        form, sigma[1], green[0], precision=highest
    )
    stacked = jnp.stack([real_part, imag_part])
    return time_step * stacked.reshape(2, item_count, window, window)


def kept_half(a, b):
    z, c = b // 2, b % 2
    return 1 - c if a < z else c if a > z else 0


def partner(a, b):
    z, c = b // 2, b % 2
    return (z, 2 * a + c) if a < z else (z, 2 * a + 1 - c)


def ways(rows_count):
    return (0, 1, rows_count // 2, rows_count // 2 + 1)


def block_plan(rows_count):
    cols_count = 2 * rows_count
    first = [[] for _ in ways(rows_count)]
    second = [[] for _ in ways(rows_count)]
    held = {}
    for a in range(rows_count):
        for b in range(cols_count):
            source = a * cols_count + b
            pa, pb = partner(a, b)
            target = pa * cols_count + pb
            for n, flip in enumerate(ways(rows_count)):
                middle = (a ^ flip) * cols_count + b
                first[n].append((source, middle))
                second[n].append((middle, target))
            keep = kept_half(a, b)
            held[(2 * a + keep, b)] = (source, 0)
            held[(2 * a + 1 - keep, b)] = (target, 1)
    return first, second, held


def split(x):
    high = x.astype(bf16)
    return high, (x - high.astype(f32)).astype(bf16)


def dot(x, y, dims=((1,), (0,))):
    return lax.dot_general(x, y, (dims, ((), ())), preferred_element_type=f32)


def dot3(x, y, dims=((1,), (0,))):
    return dot(x[0], y[0], dims) + dot(x[0], y[1], dims) + dot(x[1], y[0], dims)


def regroup(x):
    lane = lax.broadcasted_iota(jnp.int32, x[0].shape, 1)
    upper = lane >= LANES // 2
    odd = (lane // (LANES // 4)) % 2 == 1
    half, quarter = LANES // 2, LANES // 4

    def swap(p, q, mask, shift):
        return (
            jnp.where(mask, pltpu.roll(q, shift, 1), p),
            jnp.where(mask, q, pltpu.roll(p, LANES - shift, 1)),
        )

    a0, a2 = swap(x[0], x[2], upper, half)
    a1, a3 = swap(x[1], x[3], upper, half)
    y0, y1 = swap(a0, a1, odd, quarter)
    y2, y3 = swap(a2, a3, odd, quarter)
    return y0, y1, y2, y3


def send_kernel(x_ref, out_ref):
    spans = out_ref.shape[1]
    for v in range(spans):
        rows = jnp.concatenate([x_ref[0, spans * q + v] for q in range(4)], 0)
        out_ref[:, v] = rows.T.reshape(out_ref.shape[0], SUBLANES, LANES)


def pack_green(x, comp):
    _, rows, cols, momenta = x.shape
    spans = rows * cols // LANES
    devices = momenta // SUBLANES
    parts = momenta // LANES
    return pl.pallas_call(
        send_kernel,
        grid=(parts,),
        in_specs=[pl.BlockSpec((1, rows, cols, LANES), lambda p: (comp, 0, 0, p))],
        out_specs=pl.BlockSpec((devices // parts, spans, SUBLANES, LANES), lambda p: (p, 0, 0, 0)),
        out_shape=jax.ShapeDtypeStruct((devices, spans, SUBLANES, LANES), f32),
        cost_estimate=pl.CostEstimate(flops=0, bytes_accessed=x.size * 4, transcendentals=0),
        compiler_params=pltpu.CompilerParams(vmem_limit_bytes=8 * 1024 * 1024),
        name="pack_green",
    )(x)


def sigma_kernel(flags, kept_ref, re0_ref, re1_ref, im0_ref, im1_ref, fh_ref, fl_ref, ih_ref, il_ref, out_ref, plus, minus):
    points, momenta = kept_ref.shape[2], kept_ref.shape[3]
    edge = math.isqrt(points)
    spans = points // LANES
    chunk = 256
    forward = (fh_ref[...], fl_ref[...])

    half = points // 2
    pieces = (
        (0, 0, points, kept_ref.at[0, 0], kept_ref.at[1, 0]),
        (1, 0, half, re0_ref, im0_ref),
        (1, half, half, re1_ref, im1_ref),
    )
    for unit, start, count, re_ref, im_ref in pieces:

        def transform(n, carry, unit=unit, start=start, re_ref=re_ref, im_ref=im_ref):
            source = pl.ds(pl.multiple_of(n * chunk, chunk), chunk)
            rows = pl.ds(pl.multiple_of(start + n * chunk, chunk), chunk)
            y_re = dot3(split(re_ref[source, :]), forward)
            y_im = dot3(split(im_ref[source, :]), forward)
            re_c, re_s = y_re[:, :momenta], y_re[:, momenta:]
            im_c, im_s = y_im[:, :momenta], y_im[:, momenta:]
            plus[unit, 0, rows, :] = re_c - im_s
            plus[unit, 1, rows, :] = re_s + im_c
            m_re = re_c + im_s
            m_im = im_c - re_s
            for p in range(momenta // LANES):
                lanes = slice(LANES * p, LANES * (p + 1))
                minus[unit, 0, p, rows, :] = m_re[:, lanes]
                minus[unit, 1, p, rows, :] = m_im[:, lanes]
            return carry

        lax.fori_loop(0, count // chunk, transform, 0)

    inverse = (ih_ref[...], il_ref[...])
    diagonal = flags[1]
    for unit in range(2):
        facing = jnp.where(diagonal == 1, unit, 1 - unit)

        def combine(n, carry, unit=unit, facing=facing):
            s_re, s_im = [], []
            for w in range(2):
                for q in range(4):
                    i = spans * q + 2 * n + w
                    rows = pl.ds(pl.multiple_of(i * edge, edge), edge)
                    across = pl.ds(i, edge, stride=edge)
                    p_re, p_im = plus[unit, 0, rows, :], plus[unit, 1, rows, :]
                    m_re, m_im = (
                        jnp.concatenate(
                            [minus[facing, c, p, across, :] for p in range(momenta // LANES)], 1
                        )
                        for c in range(2)
                    )
                    sq_re = p_re * p_re - p_im * p_im
                    sq_im = 2.0 * p_re * p_im
                    s_re.append(sq_re * m_re - sq_im * m_im)
                    s_im.append(sq_re * m_im + sq_im * m_re)
            nt = ((1,), (1,))
            t_re = dot3(inverse, split(jnp.concatenate(s_re, 0)), nt)
            t_im = dot3(inverse, split(jnp.concatenate(s_im, 0)), nt)
            o_re = t_re[:momenta] + t_im[momenta:]
            o_im = t_im[:momenta] - t_re[momenta:]
            for w in range(2):
                lanes = slice(LANES * w, LANES * (w + 1))
                place = pl.ds(2 * n + w, SUBLANES, stride=spans)
                shape = (momenta // SUBLANES, SUBLANES, LANES)
                out_ref[:, 0, unit, place, :] = o_re[:, lanes].reshape(shape)
                out_ref[:, 1, unit, place, :] = o_im[:, lanes].reshape(shape)
            return carry

        lax.fori_loop(0, spans // 2, combine, 0)


def form_sigma(flags, x, others, tables):
    comps, _, points, momenta = x.shape
    devices = momenta // SUBLANES
    out_shape = (devices, comps, 2, SUBLANES * points // LANES, LANES)
    whole = lambda a: pl.BlockSpec(a.shape, lambda n, s: (0,) * a.ndim)
    flops = 3 * 2 * 4 * 2 * (2 * points) * momenta * momenta
    return pl.pallas_call(
        sigma_kernel,
        grid_spec=pltpu.PrefetchScalarGridSpec(
            num_scalar_prefetch=1,
            grid=(1,),
            in_specs=[
                pl.BlockSpec((comps, 1, points, momenta), lambda n, s: (0, s[0], 0, 0)),
                *[whole(t) for t in others],
                *[whole(t) for t in tables],
            ],
            out_specs=pl.BlockSpec(out_shape, lambda n, s: (0, 0, 0, 0, 0)),
            scratch_shapes=[
                pltpu.VMEM((2, comps, points, momenta), f32),
                pltpu.VMEM((2, comps, momenta // LANES, points, LANES), f32),
            ],
        ),
        out_shape=jax.ShapeDtypeStruct(out_shape, f32),
        cost_estimate=pl.CostEstimate(
            flops=flops, bytes_accessed=12 * others[0].size * 4, transcendentals=0
        ),
        compiler_params=pltpu.CompilerParams(vmem_limit_bytes=24 * 1024 * 1024),
        name="form_sigma",
    )(flags, x, *others, *tables)


def green_kernel(re_ref, im_ref, out_ref, *, rows_count):
    cols_count = 2 * rows_count
    k = pl.program_id(0)
    tile_rows = out_ref.shape[3] // rows_count
    step = tile_rows // 4
    for comp, x_ref in enumerate((re_ref, im_ref)):
        for a in range(rows_count):
            for side in range(cols_count // 4):
                groups = [[] for _ in range(4)]
                for part in range(step // SUBLANES):
                    span = pl.ds(SUBLANES * SUBLANES * part + k, SUBLANES, stride=SUBLANES)
                    loaded = [
                        x_ref[a * cols_count + 4 * side + n, span, :] for n in range(4)
                    ]
                    for q, value in enumerate(regroup(loaded)):
                        groups[q].append(value)
                for q in range(4):
                    high, low = split(jnp.concatenate(groups[q], 0))
                    rows = slice(tile_rows * a + step * q, tile_rows * a + step * (q + 1))
                    lanes = slice(LANES * side, LANES * (side + 1))
                    out_ref[0, comp, 0, rows, lanes] = high
                    out_ref[0, comp, 1, rows, lanes] = low


def arrange_green(parts, rows_count, window):
    parts = [x.reshape(x.shape[0], -1, LANES) for x in parts]
    return pl.pallas_call(
        functools.partial(green_kernel, rows_count=rows_count),
        grid=(SUBLANES,),
        in_specs=[pl.BlockSpec(x.shape, lambda k: (0, 0, 0)) for x in parts],
        out_specs=pl.BlockSpec((1, 2, 2, window, window), lambda k: (k, 0, 0, 0, 0)),
        out_shape=jax.ShapeDtypeStruct((SUBLANES, 2, 2, window, window), bf16),
        cost_estimate=pl.CostEstimate(
            flops=0, bytes_accessed=4 * parts[0].size * 4, transcendentals=0
        ),
        name="arrange_green",
    )(*parts)


def collide_kernel(s_ref, g_ref, out_ref, *lefts, held, blocks):
    window = out_ref.shape[2]
    edge = window // blocks
    for k, left in enumerate(lefts):
        for comp in range(2):
            for row in range(blocks):
                for side in range(blocks // 4):
                    loaded = []
                    for n in range(4):
                        source, unit = held[(row, 4 * side + n)]
                        loaded.append(s_ref[source, comp, unit, k])
                    high, low = split(jnp.concatenate(regroup(loaded), 0))
                    rows = slice(edge * row, edge * (row + 1))
                    lanes = slice(LANES * side, LANES * (side + 1))
                    left[comp, 0, rows, lanes] = high
                    left[comp, 1, rows, lanes] = low
        re, im = ((left[c, 0], left[c, 1]) for c in range(2))
        g_re, g_im = ((g_ref[k, c, 0], g_ref[k, c, 1]) for c in range(2))
        out_ref[0, k] = time_step * (dot3(re, g_re) - dot3(im, g_im))
        out_ref[1, k] = time_step * (dot3(re, g_im) + dot3(im, g_re))


def collide(sigma, green, held, blocks):
    window = green.shape[-1]
    rows = sigma.shape[3] // SUBLANES
    sigma = sigma.reshape(*sigma.shape[:3], SUBLANES, rows, LANES)
    return pl.pallas_call(
        functools.partial(collide_kernel, held=held, blocks=blocks),
        grid=(SUBLANES // GROUP,),
        in_specs=[
            pl.BlockSpec((*sigma.shape[:3], GROUP, rows, LANES), lambda k: (0, 0, 0, k, 0, 0)),
            pl.BlockSpec((GROUP, 2, 2, window, window), lambda k: (k, 0, 0, 0, 0)),
        ],
        out_specs=pl.BlockSpec((2, GROUP, window, window), lambda k: (0, k, 0, 0)),
        out_shape=jax.ShapeDtypeStruct((2, SUBLANES, window, window), f32),
        scratch_shapes=[pltpu.VMEM((2, 2, window, window), bf16)] * GROUP,
        cost_estimate=pl.CostEstimate(
            flops=3 * 8 * SUBLANES * window**3, bytes_accessed=3 * sigma.size * 4, transcendentals=0
        ),
        name="collide",
    )(sigma, green)


def table_pair(values):
    high = values.astype(np.float32).astype(bf16)
    low = (values - high.astype(np.float64)).astype(np.float32).astype(bf16)
    return jnp.asarray(high), jnp.asarray(low)


def dft_tables(momenta):
    index = np.arange(momenta)
    angle = 2.0 * np.pi * (index[:, None] * index[None, :] % momenta) / momenta
    cosine, sine = np.cos(angle), np.sin(angle)
    strength = coupling * coupling / momenta**3
    forward = np.concatenate([cosine, sine], 1)
    inverse = strength * np.concatenate([cosine, sine], 0)
    return (*table_pair(forward), *table_pair(inverse))


def packed_shards(green_function):
    axes = ("tr", "tc")
    rows_count = lax.axis_size("tr")
    comps, momenta, tile_rows, tile_cols = green_function.shape
    window = tile_rows * rows_count
    points = tile_cols * tile_cols
    first, second, held = block_plan(rows_count)
    a = lax.axis_index("tr")
    b = lax.axis_index("tc")
    z, c = b // 2, b % 2
    keep = jnp.where(a < z, 1 - c, jnp.where(a > z, c, 0)).astype(jnp.int32)
    diagonal = ((a == z) & (c == 0)).astype(jnp.int32)

    x = green_function.transpose(0, 2, 3, 1)
    halves = x.reshape(comps, 2, points, momenta)
    half = points // 2
    leaving = [
        lax.dynamic_slice(
            halves, (n // 2, 1 - keep, half * (n % 2), 0), (1, 1, half, momenta)
        ).reshape(half, momenta)
        for n in range(4)
    ]
    tables = dft_tables(momenta)
    others = list(leaving)
    for n in range(1, 4):
        others[n] = lax.ppermute(others[n], axes, first[n])
    for n in range(4):
        others[n] = lax.ppermute(others[n], axes, second[n])
    green = [pack_green(x, comp) for comp in range(comps)]
    for comp in range(comps):
        green[comp] = lax.all_to_all(green[comp], axes, split_axis=0, concat_axis=0, tiled=True)
    sigma = form_sigma(jnp.stack([keep, diagonal]), halves, others, tables)
    sigma = lax.all_to_all(sigma, axes, split_axis=0, concat_axis=0, tiled=True)
    green = arrange_green(green, rows_count, window)
    return collide(sigma, green, held, 2 * rows_count)


def is_packed(rows_count, cols_count, comps, momenta, tile_rows, tile_cols):
    return (
        cols_count == 2 * rows_count
        and tile_rows == 2 * tile_cols
        and 4 * tile_cols == LANES
        and momenta == SUBLANES * rows_count * cols_count
        and momenta % LANES == 0
        and cols_count % 4 == 0
        and rows_count & (rows_count - 1) == 0
    )


def shards(green_function):
    sizes = (lax.axis_size("tr"), lax.axis_size("tc"), *green_function.shape)
    return packed_shards(green_function) if is_packed(*sizes) else general_shards(green_function)


def solution(mesh):
    return jax.shard_map(
        shards,
        mesh=mesh,
        in_specs=(P(None, None, "tr", "tc"),),
        out_specs=P(None, ("tr", "tc"), None, None),
        check_vma=False,
    )
```
